512 devices in a mesh: req: 16 (over y, core), exp: 32 (over z, x).
Axes of the slice: x: 4, y: 8, z: 8, core: 2. Of those that a mesh axis runs over, the one named last changes fastest.
Arguments:
- new_q: bfloat16 [65536, 2048], P(('req', 'exp')), may hold values from -118 to 118
- new_kv: bfloat16 [65536, 4096], P(('req', 'exp')), may hold values from -4.5 to 4.5
- cache_kv: bfloat16 [65536, 4096], P(('req', 'exp')), may hold values from -4.6 to 4.6
- cache_len: int32 [512], P(('req', 'exp')), may hold values from 2 to 128
- prompt_kv: bfloat16 [4096, 4096], P(('req', 'exp')), may hold values from -4.5 to 4.5
- prompt_len: int32 [512], P(('req', 'exp')), may hold values from 1 to 8
- residual: bfloat16 [65536, 2048], P(('req', 'exp')), may hold values from -40 to 40
- norm_gain: float32 [2048], replicated, may hold values from 0.5 to 1.5
- routes: int32 [65536, 4], P(('req', 'exp')), may hold values from 0 to 31, all different within a row; in each aligned block of 128 rows (0 to 127, 128 to 255, ...) at most 20 rows name the same one
- route_weight: float32 [65536, 4], P(('req', 'exp')), may hold values from 0.1 to 1
- gate_up: bfloat16 [32, 2048, 1536], P('exp', 'req'), may hold values from -0.125 to 0.125
- down_proj: bfloat16 [32, 768, 2048], P('exp', None, 'req'), may hold values from -0.21875 to 0.21875
Outputs:
- layer_out: bfloat16 [65536, 2048], P(('req', 'exp'))
The draws below stay inside these ranges and needn't reach their ends.
Inputs may be any that keep to these rules, and one draw needn't show every extreme that they name: `routes`: each row names 4 different experts; among the rows of one request no expert is named more than 20 times.
All inputs are finite; a program needn't handle non-finite values.
Results may differ from the reference program's by a relative error of at most 0.0036.
Values may be sent and summed in bfloat16 or wider, within the bound.
A program may use at most 64 MiB of HBM per device.

```python
import functools
import math
import jax
import jax.numpy as jnp
import numpy as np
from jax import lax

D = 2048
HEADS = 16
HDIM = 128
FFE = 768
TOP = 4
GROUP = 8
TOK_DEV = 128
CMAX = 128
PSEG = 8
EXPERTS = 32
REQUESTS = 512
ROWS = 65536
CAP = 20
N_REQ = 16
N_EXP = 32


def cache_values(key):
    sampled = jax.random.truncated_normal(jax.random.fold_in(key, 11), -4.5, 4.5, (REQUESTS, CMAX, 2 * D), jnp.float32)
    return sampled


def draw_cache_kv(key, part):
    return cache_values(key).reshape(REQUESTS * CMAX, 2 * D).astype(jnp.bfloat16)


def draw_new_q(key, part):
    sampled = jax.random.truncated_normal(jax.random.fold_in(key, 12), -4.5, 4.5, (REQUESTS, TOK_DEV, D), jnp.float32)
    return sampled.reshape(REQUESTS * TOK_DEV, D).astype(jnp.bfloat16)


def draw_residual(key, part):
    row_scale = jnp.exp(jax.random.uniform(jax.random.fold_in(key, 21), (ROWS, 1), jnp.float32, 0.0, math.log(10.0)))
    col_scale = jnp.exp(jax.random.uniform(jax.random.fold_in(key, 22), (1, D), jnp.float32, 0.0, math.log(10.0)))
    texture = jax.random.truncated_normal(jax.random.fold_in(key, 23), -4.0, 4.0, (ROWS, D), jnp.float32)
    return (0.1 * texture * row_scale * col_scale).astype(jnp.bfloat16)


def draw_cache_len(key, part):
    counts = jax.random.randint(jax.random.fold_in(key, 31), (REQUESTS,), 2, CMAX + 1)
    full_at = jax.random.randint(jax.random.fold_in(key, 32), (), 0, REQUESTS)
    return counts.at[full_at].set(CMAX).astype(jnp.int32)


def draw_prompt_len(key, part):
    counts = jax.random.randint(jax.random.fold_in(key, 41), (REQUESTS,), 1, PSEG + 1)
    full_at = jax.random.randint(jax.random.fold_in(key, 42), (), 0, REQUESTS)
    return counts.at[full_at].set(PSEG).astype(jnp.int32)


def block_levels(stream_key, dims, shards, smallest, high):
    def one(position, shards_of):
        steps = jax.random.uniform(jax.random.fold_in(jax.random.fold_in(stream_key, 6), position), (shards_of,), jnp.float32, smallest / len(shards), high / len(shards))
        return jnp.repeat(jnp.exp(steps), dims[position] // shards_of).reshape((-1,) + (1,) * (len(dims) - position - 1))

    factor_of = one(*shards[0])
    for cut in shards[1:]:
        factor_of = factor_of * one(*cut)
    return factor_of


def assign_block(key, own, number, rows, amount, top, most, skew):
    order = jax.random.permutation(key, amount)
    heavy_load, ordinary = load_shares(amount, rows * top, most, skew, True), load_shares(amount, rows * top, most, skew, False)
    places = jnp.arange(amount)

    def named(tallies, turn):
        used = int((tallies > 0).sum())
        fixed = max(1, used // 4)
        passed = fixed + (places - fixed + turn * (used - fixed)) % max(1, amount - fixed)
        return jnp.zeros((amount,), jnp.int32).at[order[jnp.where(places < fixed, places, passed)]].set(jnp.asarray(tallies, jnp.int32))

    tallies = jnp.where(number % 4 == 0, named(heavy_load, number // 4), named(ordinary, number - number // 4 - 1))
    mixed = jax.random.permutation(jax.random.fold_in(own, 3), amount)
    source_of, sink = mixed[0:amount // 2 * 2:2], mixed[1:amount // 2 * 2:2]
    margin = jnp.minimum(tallies[source_of] - 1, most - tallies[sink]) // 2
    margin = jnp.where((source_of == order[0]) | (sink == order[0]) | (tallies[sink] == 0), 0, jnp.maximum(margin, 0))
    passed = jax.random.randint(jax.random.fold_in(own, 4), (amount // 2,), 0, 1 << 20) % (margin + 1)
    tallies = tallies.at[source_of].add(-passed).at[sink].add(passed)
    labels = jnp.searchsorted(jnp.cumsum(tallies), jnp.arange(rows * top), side="right").astype(jnp.int32)
    listing = labels.reshape(top, rows).T
    listing = listing[jax.random.permutation(jax.random.fold_in(own, 1), rows)]
    turn = jax.random.randint(jax.random.fold_in(own, 2), (rows, 1), 0, top)
    return jnp.take_along_axis(listing, (jnp.arange(top)[None, :] + turn) % top, axis=1)


def load_shares(amount, total, most, lean, full):
    portions = [(1 << 20) // math.isqrt(standing ** lean) + 1 for standing in range(1, amount + 1)]
    largest = most if full else min(most, max(-(-total // amount), total * portions[0] // sum(portions)))
    least = 1 if total - largest >= amount - 1 else 0
    given, spare = [largest] + [least] * (amount - 1), total - largest - least * (amount - 1)
    while spare > 0:
        movable = [i for i in range(1, amount) if given[i] < largest] or [i for i in range(1, amount) if given[i] < most]
        mass, budget = sum([portions[i] for i in movable]), spare
        for i in movable:
            addition = min(most - given[i], max(1, budget * portions[i] // mass), spare)
            given[i] = given[i] + addition
            spare = spare - addition
    return np.array(given)


def scatter_about(stream_key, dims, width, most, shards=(), kind=jnp.bfloat16):
    drawn = jax.random.normal(stream_key, dims, jnp.float32) * width
    if len(shards) > 0:
        drawn = block_levels(stream_key, dims, shards, -0.22, 0.18) * drawn
    return jnp.clip(drawn, min=-most, max=most).astype(kind)


def setup_inputs(seed: int = 0) -> dict:
    streams_of = jax.random.split(jax.random.key(seed), 13)
    new_q = draw_new_q(jax.random.fold_in(streams_of[12], 71), 0)
    new_kv = scatter_about(streams_of[1], (ROWS, 2 * D), 1.0, 4.5, ((0, 512),))
    cache_kv = draw_cache_kv(jax.random.fold_in(streams_of[12], 71), 0)
    cache_len = draw_cache_len(jax.random.fold_in(streams_of[12], 71), 0)
    prompt_kv = scatter_about(streams_of[4], (REQUESTS * PSEG, 2 * D), 1.0, 4.5, ((0, 512),))
    prompt_len = draw_prompt_len(jax.random.fold_in(streams_of[12], 71), 0)
    residual = draw_residual(jax.random.fold_in(streams_of[12], 71), 0)
    norm_gain = jnp.clip(1.0 + 0.1 * jax.random.normal(streams_of[7], (D,), jnp.float32), 0.5, 1.5)
    routes_keys = jax.random.split(jax.random.fold_in(streams_of[8], 1), ROWS // TOK_DEV)
    routes_turns = jax.random.permutation(jax.random.fold_in(streams_of[8], 3), ROWS // TOK_DEV)
    routes = jax.vmap(lambda own, number: assign_block(jax.random.fold_in(streams_of[8], 2), own, number, TOK_DEV, EXPERTS, TOP, CAP, 2))(routes_keys, routes_turns).reshape((ROWS, TOP))
    route_weight = jnp.clip(jnp.exp(math.log(1.0) - 2.3025851 * jax.random.uniform(streams_of[9], (ROWS, TOP), jnp.float32) ** block_levels(streams_of[9], (ROWS, TOP), ((0, 512),), -0.2, 0.2)), 0.1, 1.0)
    gate_up = scatter_about(streams_of[10], (EXPERTS, D, 2 * FFE), D ** -0.5, 0.125, ((0, 32), (1, 16)))
    down_proj = scatter_about(streams_of[11], (EXPERTS, FFE, D), FFE ** -0.5, 0.21875, ((0, 32), (2, 16)))
    return {"new_q": new_q, "new_kv": new_kv, "cache_kv": cache_kv, "cache_len": cache_len, "prompt_kv": prompt_kv, "prompt_len": prompt_len, "residual": residual, "norm_gain": norm_gain, "routes": routes, "route_weight": route_weight, "gate_up": gate_up, "down_proj": down_proj}


eps_norm = 1e-06

def route_slots(route_ids, expert_count):
    flat_ids = route_ids.reshape(-1).astype(jnp.int32)
    expert_iota = jnp.arange(expert_count, dtype=jnp.int32)
    one_hot = (flat_ids[:, None] == expert_iota[None, :]).astype(jnp.int32)
    earlier = (jnp.cumsum(one_hot, axis=0) - one_hot).astype(jnp.int32)
    slot_ids = lax.optimization_barrier(jnp.sum(earlier * one_hot, axis=1)).astype(jnp.int32)
    return (flat_ids, slot_ids)

def pack_slots(normed, flat_ids, slot_ids, expert_count, capacity):
    token_count = normed.shape[0]
    pair_tokens = (jnp.arange(flat_ids.shape[0], dtype=jnp.int32) // TOP).astype(jnp.int32)
    where_to = (flat_ids * capacity + slot_ids).astype(jnp.int32)
    source_row = jnp.full((expert_count * capacity,), token_count, jnp.int32).at[where_to].set(pair_tokens)
    padded = jnp.concatenate([normed, jnp.zeros((1, normed.shape[1]), normed.dtype)], axis=0)
    return padded[source_row].reshape(expert_count, capacity, normed.shape[1])

def attend_ref(query, own_kv, own_cache, cache_count, group_kv, group_count):
    tok_count = query.shape[0]
    seg_rows = group_kv.shape[0] // GROUP
    prompt_ok = jnp.arange(GROUP * seg_rows, dtype=jnp.int32) % seg_rows < jnp.repeat(group_count, seg_rows)
    cache_ok = jnp.arange(own_cache.shape[0], dtype=jnp.int32) < cache_count
    fixed_ok = jnp.concatenate([prompt_ok, cache_ok])
    positions = jnp.arange(tok_count, dtype=jnp.int32)
    causal = positions[None, :] <= positions[:, None]
    visible = jnp.concatenate([jnp.broadcast_to(fixed_ok[None, :], (tok_count, fixed_ok.shape[0])), causal], axis=1)
    keys_values = jnp.concatenate([group_kv, own_cache, own_kv], axis=0)
    model_width = query.shape[1]
    queries = query.astype(jnp.float32).reshape(tok_count, HEADS, HDIM)
    key_heads = keys_values[:, :model_width].astype(jnp.float32).reshape(-1, HEADS, HDIM)
    value_heads = keys_values[:, model_width:].astype(jnp.float32).reshape(-1, HEADS, HDIM)
    scores = jnp.einsum('qhd,khd->hqk', queries, key_heads) / math.sqrt(HDIM)
    scores = jnp.where(visible[None], scores, -jnp.inf)
    row_peak = lax.optimization_barrier(jnp.max(scores, axis=2, keepdims=True))
    weights = jnp.exp(scores - row_peak)
    totals = lax.optimization_barrier(jnp.sum(weights, axis=2))
    rounded_probs = lax.optimization_barrier(weights.astype(jnp.bfloat16)).astype(jnp.float32)
    summed = jnp.einsum('hqk,khd->qhd', rounded_probs, value_heads)
    attended = summed / jnp.transpose(totals)[:, :, None]
    return attended.reshape(tok_count, model_width).astype(jnp.bfloat16)

def norm_rows(stream, gain_row):
    mean_sq = lax.optimization_barrier(jnp.mean(stream * stream, axis=1, keepdims=True))
    return (stream * lax.rsqrt(mean_sq + eps_norm) * gain_row[None, :]).astype(jnp.bfloat16)

def activate(gate_up_out):
    half_width = gate_up_out.shape[-1] // 2
    return (jax.nn.silu(gate_up_out[..., :half_width]) * gate_up_out[..., half_width:]).astype(jnp.bfloat16)

def combine_rows(returned, flat_ids, slot_ids, stream, weight_rows):
    chosen = returned.reshape(-1, D)[flat_ids * CAP + slot_ids].astype(jnp.float32)
    chosen = chosen.reshape(TOK_DEV, TOP, D)
    return (stream + lax.optimization_barrier(jnp.sum(chosen * weight_rows[:, :, None], axis=1))).astype(jnp.bfloat16)

def reference(new_q, new_kv, cache_kv, cache_len, prompt_kv, prompt_len, residual, norm_gain, routes, route_weight, gate_up, down_proj):
    group_total = N_EXP // GROUP
    query_groups = new_q.reshape(N_REQ, N_EXP, TOK_DEV, D)
    new_groups = new_kv.reshape(N_REQ, N_EXP, TOK_DEV, 2 * D)
    cache_groups = cache_kv.reshape(N_REQ, N_EXP, CMAX, 2 * D)
    cache_counts = cache_len.reshape(N_REQ, N_EXP)
    prompt_groups = prompt_kv.reshape(N_REQ, group_total, GROUP * PSEG, 2 * D)
    prompt_counts = prompt_len.reshape(N_REQ, group_total, GROUP)
    residual_groups = residual.reshape(N_REQ, N_EXP, TOK_DEV, D)
    route_groups = routes.reshape(N_REQ, N_EXP, TOK_DEV, TOP)
    weight_groups = route_weight.reshape(N_REQ, N_EXP, TOK_DEV, TOP)
    gate_up_wide = gate_up.astype(jnp.float32)
    down_wide = down_proj.astype(jnp.float32)
    slot_fn = functools.partial(route_slots, expert_count=EXPERTS)
    pack_fn = functools.partial(pack_slots, expert_count=EXPERTS, capacity=CAP)

    def one_group(inputs):
        query_g, new_g, cache_g, count_g, prompt_g, plen_g, resid_g, route_g, weight_g = inputs
        group_of = (jnp.arange(N_EXP, dtype=jnp.int32) // GROUP).astype(jnp.int32)
        prompt_each = prompt_g[group_of]
        plen_each = plen_g[group_of]
        attended = jax.vmap(attend_ref)(query_g, new_g, cache_g, count_g, prompt_each, plen_each)
        stream = resid_g.astype(jnp.float32) + attended.astype(jnp.float32)
        normed = jax.vmap(norm_rows, in_axes=(0, None))(stream, norm_gain)
        flat_ids, slot_ids = jax.vmap(slot_fn)(route_g)
        outbox = pack_fn_v(normed, flat_ids, slot_ids)
        arrived = jnp.transpose(outbox, (1, 0, 2, 3)).reshape(EXPERTS, N_EXP * CAP, D)
        arrived = lax.optimization_barrier(arrived).astype(jnp.float32)
        gate_up_out = jnp.einsum('esd,edf->esf', arrived, gate_up_wide)
        activated = lax.optimization_barrier(activate(gate_up_out)).astype(jnp.float32)
        expert_out = jnp.einsum('esf,efd->esd', activated, down_wide).astype(jnp.bfloat16)
        returned = jnp.transpose(expert_out.reshape(EXPERTS, N_EXP, CAP, D), (1, 0, 2, 3))
        return jax.vmap(combine_rows)(returned, flat_ids, slot_ids, stream, weight_g)
    pack_fn_v = jax.vmap(pack_fn)
    outputs = lax.map(one_group, (query_groups, new_groups, cache_groups, cache_counts, prompt_groups, prompt_counts, residual_groups, route_groups, weight_groups))
    return outputs.reshape(ROWS, D)
```

```python
import math

import jax
import jax.numpy as jnp
from jax import lax
from jax.sharding import PartitionSpec as P

HEADS = 16
HDIM = 128
TOP = 4
GROUP = 8


eps_norm = 1e-06


HALVES = 2
SUB = 8


def gather_prompt(prompt_kv, prompt_len):
    rows = prompt_kv.shape[0]
    count_cols = jnp.broadcast_to(prompt_len.astype(jnp.bfloat16)[:, None], (rows, HDIM))
    block = jnp.concatenate([prompt_kv, count_cols], axis=1)
    axis_total = lax.axis_size("exp")
    parts = [block]
    for offset in range(1, GROUP):
        route = [(one, one ^ offset) for one in range(axis_total)]
        parts.append(lax.ppermute(block, "exp", route))
    gathered = jnp.concatenate(parts, axis=0)
    width = prompt_kv.shape[1]
    row_counts = gathered[:, width].astype(jnp.int32)
    row_index = jnp.arange(GROUP * rows, dtype=jnp.int32) % rows
    return gathered[:, :width], row_index < row_counts


def slot_layout(expert_count, capacity):
    main = capacity // SUB * SUB
    rest = capacity - main
    block = HALVES * capacity
    row = jnp.arange(expert_count * block, dtype=jnp.int32)
    expert = row // block
    inner = row % block
    in_main = inner < HALVES * main
    left_over = inner - HALVES * main
    half = jnp.where(in_main, inner // main, left_over // rest)
    slot = jnp.where(in_main, inner % main, main + left_over % rest)
    spread = (jnp.arange(expert_count, dtype=jnp.int32)[:, None] == expert[None, :]).astype(
        jnp.bfloat16
    )
    return spread, half, slot


def membership(routes, expert_count):
    experts = jnp.arange(expert_count, dtype=jnp.int32)
    return routes[:, :, None] == experts[None, None, :]


def slot_codes(chosen, spread):
    member = jnp.any(chosen, axis=1)
    tok_count = member.shape[0]
    order = jnp.arange(tok_count, dtype=jnp.int32)
    up_to = (order[None, :] <= order[:, None]).astype(jnp.bfloat16)
    upto_count = jnp.dot(
        up_to, member.astype(jnp.bfloat16), preferred_element_type=jnp.float32
    )
    codes = jnp.where(member, upto_count, 0.0).astype(jnp.bfloat16)
    return jnp.dot(codes, spread, preferred_element_type=jnp.float32).astype(jnp.bfloat16)


def pack_slots(normed, codes, half, slot):
    width = normed.shape[1] // HALVES
    wanted = (slot + 1).astype(jnp.bfloat16)
    picks = [
        jnp.where((half == which)[None, :] & (codes == wanted[None, :]), 1.0, 0.0).astype(
            jnp.bfloat16
        )
        for which in range(HALVES)
    ]
    stacked = jnp.concatenate(
        [normed[:, which * width : (which + 1) * width] for which in range(HALVES)], axis=0
    )
    return lax.dot_general(
        jnp.concatenate(picks, axis=0),
        stacked,
        (((0,), (0,)), ((), ())),
        preferred_element_type=jnp.float32,
    ).astype(jnp.bfloat16)


def combine_rows(returned, chosen, route_weight, codes, spread, half, slot):
    tok_count = route_weight.shape[0]
    by_expert = jnp.sum(jnp.where(chosen, route_weight[:, :, None], 0.0), axis=1)
    high = by_expert.astype(jnp.bfloat16)
    low = (by_expert - high.astype(jnp.float32)).astype(jnp.bfloat16)
    wide = jnp.dot(
        jnp.concatenate([high, low], axis=0), spread, preferred_element_type=jnp.float32
    ).astype(jnp.bfloat16)
    wanted = (slot + 1).astype(jnp.bfloat16)
    hit = codes == wanted[None, :]
    hits = jnp.concatenate([hit, hit], axis=0)
    mixes = [
        jnp.where((half == which)[None, :] & hits, wide, 0.0).astype(jnp.bfloat16)
        for which in range(HALVES)
    ]
    summed = jnp.dot(
        jnp.concatenate(mixes, axis=0), returned, preferred_element_type=jnp.float32
    )
    pieces = [
        summed[2 * which * tok_count : (2 * which + 1) * tok_count]
        + summed[(2 * which + 1) * tok_count : (2 * which + 2) * tok_count]
        for which in range(HALVES)
    ]
    return jnp.concatenate(pieces, axis=1)


def attend_local(query, own_kv, own_cache, cache_count, group_kv, prompt_ok):
    tok_count = query.shape[0]
    cache_ok = jnp.arange(own_cache.shape[0], dtype=jnp.int32) < cache_count
    fixed_ok = jnp.concatenate([prompt_ok, cache_ok])
    positions = jnp.arange(tok_count, dtype=jnp.int32)
    causal = positions[None, :] <= positions[:, None]
    visible = jnp.concatenate(
        [jnp.broadcast_to(fixed_ok[None, :], (tok_count, fixed_ok.shape[0])), causal], axis=1
    )
    keys_values = jnp.concatenate([group_kv, own_cache, own_kv], axis=0)
    model_width = query.shape[1]
    queries = query.reshape(tok_count, HEADS, HDIM)
    key_heads = keys_values[:, :model_width].reshape(-1, HEADS, HDIM)
    value_heads = keys_values[:, model_width:].reshape(-1, HEADS, HDIM)
    scores = jnp.einsum(
        "qhd,khd->hqk", queries, key_heads, preferred_element_type=jnp.float32
    ) / math.sqrt(HDIM)
    scores = jnp.where(visible[None], scores, -jnp.inf)
    row_peak = jnp.max(scores, axis=2, keepdims=True)
    weights = jnp.exp(scores - row_peak)
    totals = jnp.sum(weights, axis=2)
    rounded_probs = weights.astype(jnp.bfloat16)
    summed = jnp.einsum(
        "hqk,khd->qhd", rounded_probs, value_heads, preferred_element_type=jnp.float32
    )
    attended = summed / jnp.transpose(totals)[:, :, None]
    return attended.reshape(tok_count, model_width).astype(jnp.bfloat16)


def norm_rows(stream, gain_row):
    mean_sq = jnp.mean(stream * stream, axis=1, keepdims=True)
    return (stream * lax.rsqrt(mean_sq + eps_norm) * gain_row[None, :]).astype(jnp.bfloat16)


def activate(gate_up_out):
    half_width = gate_up_out.shape[-1] // 2
    return (jax.nn.silu(gate_up_out[..., :half_width]) * gate_up_out[..., half_width:]).astype(
        jnp.bfloat16
    )


def expert_local(arrived, rows_weight, cols_weight):
    sources, block, width = arrived.shape
    main = block // HALVES // SUB * SUB
    rest = block // HALVES - main
    tail = arrived[:, HALVES * main :]
    swapped = jnp.concatenate([tail[:, rest:], tail[:, :rest]], axis=1)
    left = jnp.concatenate([arrived[:, :main], tail], axis=1)
    right = jnp.concatenate([arrived[:, main : HALVES * main], swapped], axis=1)
    flat_rows = jnp.concatenate([left, right], axis=2).reshape(-1, HALVES * width)
    gate_up_out = jnp.dot(flat_rows, rows_weight, preferred_element_type=jnp.float32)
    activated = activate(gate_up_out)
    result = jnp.dot(activated, cols_weight, preferred_element_type=jnp.float32).astype(
        jnp.bfloat16
    )
    result = result.reshape(sources, main + HALVES * rest, HALVES * width)
    return jnp.concatenate(
        [
            result[:, :main, :width],
            result[:, :main, width:],
            result[:, main : main + rest, :width],
            result[:, main : main + rest, width:],
        ],
        axis=1,
    )


def body(
    new_q,
    new_kv,
    cache_kv,
    cache_len,
    prompt_kv,
    prompt_len,
    residual,
    norm_gain,
    routes,
    route_weight,
    gate_up,
    down_proj,
):
    group_kv, prompt_ok = gather_prompt(prompt_kv, prompt_len)
    experts_here = lax.axis_size("exp")
    token_count = new_q.shape[0]
    capacity = token_count * TOP * 5 // (4 * experts_here)
    spread, half, slot = slot_layout(experts_here, capacity)
    chosen = membership(routes, experts_here)
    codes = slot_codes(chosen, spread)
    rows_weight, cols_weight = (
        lax.all_gather(gate_up[0], "req", axis=0, tiled=True),
        lax.all_gather(down_proj[0], "req", axis=1, tiled=True),
    )
    attended = attend_local(new_q, new_kv, cache_kv, cache_len[0], group_kv, prompt_ok)
    stream = residual.astype(jnp.float32) + attended.astype(jnp.float32)
    normed = norm_rows(stream, norm_gain)
    outbox = pack_slots(normed, codes, half, slot)
    outbox = outbox.reshape(experts_here, HALVES * capacity, -1)
    arrived = lax.all_to_all(outbox, "exp", split_axis=0, concat_axis=0, tiled=True)
    returned = lax.all_to_all(
        expert_local(arrived, rows_weight, cols_weight),
        "exp",
        split_axis=0,
        concat_axis=0,
        tiled=True,
    )
    returned = returned.reshape(-1, returned.shape[-1])
    combined = combine_rows(returned, chosen, route_weight, codes, spread, half, slot)
    return (stream + combined).astype(jnp.bfloat16)


def solution(mesh):
    return jax.shard_map(
        body,
        mesh=mesh,
        in_specs=(
            P(("req", "exp"), None),
            P(("req", "exp"), None),
            P(("req", "exp"), None),
            P(("req", "exp")),
            P(("req", "exp"), None),
            P(("req", "exp")),
            P(("req", "exp"), None),
            P(),
            P(("req", "exp"), None),
            P(("req", "exp"), None),
            P("exp", "req", None),
            P("exp", None, "req"),
        ),
        out_specs=P(("req", "exp"), None),
        check_vma=False,
    )
```

```python
import math

import jax
import jax.numpy as jnp
import numpy as np
from jax import lax
from jax.experimental import pallas as pl
from jax.experimental.pallas import tpu as pltpu
from jax.sharding import PartitionSpec as P

HEADS = 16
HDIM = 128
TOP = 4
GROUP = 8


eps_norm = 1e-06


HALVES = 2
SUB = 8


def slot_layout(expert_count, capacity):
    main = capacity // SUB * SUB
    rest = capacity - main
    block = HALVES * capacity
    row = jnp.arange(expert_count * block, dtype=jnp.int32)
    expert = row // block
    inner = row % block
    in_main = inner < HALVES * main
    left_over = inner - HALVES * main
    half = jnp.where(in_main, inner // main, left_over // rest)
    slot = jnp.where(in_main, inner % main, main + left_over % rest)
    spread = (jnp.arange(expert_count, dtype=jnp.int32)[:, None] == expert[None, :]).astype(
        jnp.bfloat16
    )
    return spread, half, slot


def membership(routes, expert_count):
    experts = jnp.arange(expert_count, dtype=jnp.int32)
    return routes[:, :, None] == experts[None, None, :]


def slot_codes(chosen, spread):
    member = jnp.any(chosen, axis=1)
    tok_count = member.shape[0]
    order = jnp.arange(tok_count, dtype=jnp.int32)
    up_to = (order[None, :] <= order[:, None]).astype(jnp.bfloat16)
    upto_count = jnp.dot(
        up_to, member.astype(jnp.bfloat16), preferred_element_type=jnp.float32
    )
    codes = jnp.where(member, upto_count, 0.0).astype(jnp.bfloat16)
    return jnp.dot(codes, spread, preferred_element_type=jnp.float32).astype(jnp.bfloat16)


def combine_rows(returned, chosen, route_weight, codes, spread, half, slot):
    tok_count = route_weight.shape[0]
    by_expert = jnp.sum(jnp.where(chosen, route_weight[:, :, None], 0.0), axis=1)
    high = by_expert.astype(jnp.bfloat16)
    low = (by_expert - high.astype(jnp.float32)).astype(jnp.bfloat16)
    wide = jnp.dot(
        jnp.concatenate([high, low], axis=0), spread, preferred_element_type=jnp.float32
    ).astype(jnp.bfloat16)
    wanted = (slot + 1).astype(jnp.bfloat16)
    hit = codes == wanted[None, :]
    hits = jnp.concatenate([hit, hit], axis=0)
    mixes = [
        jnp.where((half == which)[None, :] & hits, wide, 0.0).astype(jnp.bfloat16)
        for which in range(HALVES)
    ]
    summed = jnp.dot(
        jnp.concatenate(mixes, axis=0), returned, preferred_element_type=jnp.float32
    )
    pieces = [
        summed[2 * which * tok_count : (2 * which + 1) * tok_count]
        + summed[(2 * which + 1) * tok_count : (2 * which + 2) * tok_count]
        for which in range(HALVES)
    ]
    return jnp.concatenate(pieces, axis=1)


def slot_tables(expert_count, capacity):
    main = capacity // SUB * SUB
    rest = capacity - main
    block = HALVES * capacity
    row = np.arange(expert_count * block)
    inner = row % block
    in_main = inner < HALVES * main
    left_over = inner - HALVES * main
    half = np.where(in_main, inner // main, left_over // rest)
    slot = np.where(in_main, inner % main, main + left_over % rest)
    spread = (np.arange(expert_count)[None, :] == (row // block)[:, None]).astype(np.float32)
    wanted = np.stack(
        [np.where(half == which, slot + 1, -1) for which in range(HALVES)], axis=1
    ).astype(np.float32)
    return spread, wanted


NT = (((1,), (1,)), ((), ()))


def attend_kernel(
    count_ref,
    query_ref,
    own_ref,
    cache_ref,
    block_ref,
    residual_ref,
    gain_ref,
    routes_ref,
    spread_ref,
    wanted_ref,
    stream_ref,
    outbox_ref,
    far_ref,
    local_ref,
    send_sem,
    recv_sem,
):
    tok_count, width = query_ref.shape
    heads = width // HDIM
    experts = spread_ref.shape[1]
    position = lax.axis_index("exp")
    base = position // GROUP * GROUP
    rank = position - base
    barrier = pltpu.get_barrier_semaphore()
    for offset in range(1, GROUP):
        pl.semaphore_signal(
            barrier,
            inc=1,
            device_id={"exp": base + (rank + offset) % GROUP},
            device_id_type=pl.DeviceIdType.MESH,
        )
    pl.semaphore_wait(barrier, GROUP - 1)
    copies = []
    for offset in range(1, GROUP):
        copy = pltpu.make_async_remote_copy(
            src_ref=block_ref,
            dst_ref=far_ref.at[offset - 1],
            send_sem=send_sem.at[offset - 1],
            recv_sem=recv_sem.at[offset - 1],
            device_id={"exp": base + (rank + offset) % GROUP},
            device_id_type=pl.DeviceIdType.MESH,
        )
        copy.start()
        copies.append(copy)

    scale = 1.0 / math.sqrt(HDIM)
    rows = lax.broadcasted_iota(jnp.int32, (tok_count, tok_count), 0)
    cols = lax.broadcasted_iota(jnp.int32, (tok_count, tok_count), 1)
    causal = cols <= rows
    live = lax.broadcasted_iota(jnp.int32, (tok_count, cache_ref.shape[0]), 1) < count_ref[0]
    peaks = []
    sums = []
    for head in range(heads):
        at = slice(head * HDIM, (head + 1) * HDIM)
        values_at = slice(width + head * HDIM, width + (head + 1) * HDIM)
        query = query_ref[:, at]
        own = lax.dot_general(query, own_ref[:, at], NT, preferred_element_type=jnp.float32)
        old = lax.dot_general(query, cache_ref[:, at], NT, preferred_element_type=jnp.float32)
        own = jnp.where(causal, own * scale, -jnp.inf)
        old = jnp.where(live, old * scale, -jnp.inf)
        peak = jnp.max(jnp.maximum(own, old), axis=1, keepdims=True)
        own = jnp.exp(own - peak)
        old = jnp.exp(old - peak)
        sums.append(jnp.sum(own + old, axis=1, keepdims=True))
        peaks.append(peak)
        local_ref[:, at] = jnp.dot(
            own.astype(jnp.bfloat16), own_ref[:, values_at], preferred_element_type=jnp.float32
        ) + jnp.dot(
            old.astype(jnp.bfloat16), cache_ref[:, values_at], preferred_element_type=jnp.float32
        )

    lanes = lax.broadcasted_iota(jnp.int32, (tok_count, experts), 1)
    member = jnp.zeros((tok_count, experts), jnp.float32)
    for k in range(TOP):
        member = member + jnp.where(routes_ref[:, k : k + 1] == lanes, 1.0, 0.0)
    ranks = jnp.dot(
        jnp.where(causal, 1.0, 0.0).astype(jnp.bfloat16),
        member.astype(jnp.bfloat16),
        preferred_element_type=jnp.float32,
    )
    codes = (ranks * member).astype(jnp.bfloat16)
    codes = lax.dot_general(spread_ref[...], codes, NT, preferred_element_type=jnp.float32)
    picks = [
        jnp.where(codes == wanted_ref[:, which : which + 1], 1.0, 0.0).astype(jnp.bfloat16)
        for which in range(HALVES)
    ]

    for copy in copies:
        copy.wait()
    prompt_rows = block_ref.shape[0]
    far = jnp.concatenate([block_ref[...][None], far_ref[...]], axis=0)
    in_segment = lax.broadcasted_iota(jnp.int32, (GROUP, prompt_rows, HDIM), 1)
    dead = jnp.where(
        in_segment.astype(jnp.float32) < far[:, :, 2 * width :].astype(jnp.float32), 0.0, 1.0
    )
    keys_total = GROUP * prompt_rows
    dead = dead.reshape(keys_total, HDIM).astype(jnp.bfloat16)
    far = far.reshape(keys_total, far.shape[2])
    ones = jnp.full((tok_count, HDIM), 1.0 / HDIM, jnp.bfloat16)
    hidden = lax.dot_general(ones, dead, NT, preferred_element_type=jnp.float32) > 0.5
    squares = jnp.zeros((tok_count, HDIM), jnp.float32)
    for head in range(heads):
        at = slice(head * HDIM, (head + 1) * HDIM)
        values_at = slice(width + head * HDIM, width + (head + 1) * HDIM)
        scores = lax.dot_general(
            query_ref[:, at], far[:, at], NT, preferred_element_type=jnp.float32
        )
        scores = jnp.where(hidden, -jnp.inf, scores * scale)
        peak = jnp.maximum(peaks[head], jnp.max(scores, axis=1, keepdims=True))
        shrink = jnp.exp(peaks[head] - peak)
        weights = jnp.exp(scores - peak)
        total = sums[head] * shrink + jnp.sum(weights, axis=1, keepdims=True)
        summed = local_ref[:, at] * shrink + jnp.dot(
            weights.astype(jnp.bfloat16), far[:, values_at], preferred_element_type=jnp.float32
        )
        attended = (summed / total).astype(jnp.bfloat16).astype(jnp.float32)
        stream = residual_ref[:, at].astype(jnp.float32) + attended
        stream_ref[:, at] = stream
        squares = squares + stream * stream
    mean_sq = jnp.sum(squares, axis=1, keepdims=True) / width
    normed = (stream_ref[...] * lax.rsqrt(mean_sq + eps_norm) * gain_ref[...]).astype(jnp.bfloat16)
    part = width // HALVES
    outbox_ref[...] = (
        jnp.dot(picks[0], normed[:, :part], preferred_element_type=jnp.float32)
        + jnp.dot(picks[1], normed[:, part:], preferred_element_type=jnp.float32)
    ).astype(jnp.bfloat16)


def attend_and_pack(
    query, own_kv, own_cache, cache_count, prompt_kv, prompt_len, residual, gain, routes, experts, capacity
):
    tok_count, width = query.shape
    prompt_rows = prompt_kv.shape[0]
    count_cols = jnp.broadcast_to(prompt_len.astype(jnp.bfloat16)[:, None], (prompt_rows, HDIM))
    block = jnp.concatenate([prompt_kv, count_cols], axis=1)
    spread, wanted = slot_tables(experts, capacity)
    vmem = pl.BlockSpec(memory_space=pltpu.VMEM)
    slots = experts * HALVES * capacity
    return pl.pallas_call(
        attend_kernel,
        out_shape=(
            jax.ShapeDtypeStruct((tok_count, width), jnp.float32),
            jax.ShapeDtypeStruct((slots, width // HALVES), jnp.bfloat16),
        ),
        in_specs=[pl.BlockSpec(memory_space=pltpu.SMEM)] + [vmem] * 9,
        out_specs=(vmem, vmem),
        scratch_shapes=[
            pltpu.VMEM((GROUP - 1,) + block.shape, jnp.bfloat16),
            pltpu.VMEM((tok_count, width), jnp.float32),
            pltpu.SemaphoreType.DMA((GROUP - 1,)),
            pltpu.SemaphoreType.DMA((GROUP - 1,)),
        ],
        compiler_params=pltpu.CompilerParams(
            collective_id=0, has_side_effects=True, vmem_limit_bytes=40 * 1024 * 1024
        ),
        cost_estimate=pl.CostEstimate(
            flops=2 * 10**9, bytes_accessed=8 * 10**6, transcendentals=655360
        ),
    )(
        cache_count,
        query,
        own_kv,
        own_cache,
        block,
        residual,
        gain[None, :],
        routes,
        jnp.asarray(spread, jnp.bfloat16),
        jnp.asarray(wanted),
    )


def expert_kernel(arrived_ref, gate_ref, up_ref, down_ref, out_ref, rows_ref, total_ref):
    step = pl.program_id(0)
    sources, block, width = arrived_ref.shape
    main = block // HALVES // SUB * SUB
    rest = block // HALVES - main
    tall = sources * main

    @pl.when(step == 0)
    def _():
        rows_ref[:tall, :width] = arrived_ref[:, :main, :].reshape(tall, width)
        rows_ref[:tall, width:] = arrived_ref[:, main : HALVES * main, :].reshape(tall, width)
        tail = arrived_ref[:, HALVES * main :, :].astype(jnp.float32)
        swapped = jnp.concatenate([tail[:, rest:], tail[:, :rest]], axis=1)
        rows_ref[tall:, :width] = tail.reshape(-1, width).astype(jnp.bfloat16)
        rows_ref[tall:, width:] = swapped.reshape(-1, width).astype(jnp.bfloat16)

    rows = rows_ref[...]
    gate = jnp.dot(rows, gate_ref[...], preferred_element_type=jnp.float32)
    up = jnp.dot(rows, up_ref[...], preferred_element_type=jnp.float32)
    activated = (gate / (1.0 + jnp.exp(-gate)) * up).astype(jnp.bfloat16)
    result = jnp.dot(activated, down_ref[...], preferred_element_type=jnp.float32)

    @pl.when(step == 0)
    def _():
        total_ref[...] = result

    @pl.when(step > 0)
    def _():
        total_ref[...] = total_ref[...] + result

    @pl.when(step == pl.num_programs(0) - 1)
    def _():
        out_ref[:, :main, :] = (
            total_ref[:tall, :width].astype(jnp.bfloat16).reshape(sources, main, width)
        )
        out_ref[:, main : HALVES * main, :] = (
            total_ref[:tall, width:].astype(jnp.bfloat16).reshape(sources, main, width)
        )
        left = total_ref[tall:, :width].reshape(sources, HALVES * rest, width)
        right = total_ref[tall:, width:].reshape(sources, HALVES * rest, width)
        out_ref[:, HALVES * main :, :] = jnp.concatenate(
            [left[:, :rest], right[:, :rest]], axis=1
        ).astype(jnp.bfloat16)


def expert_local(arrived, rows_weight, cols_weight):
    sources, block, width = arrived.shape
    main = block // HALVES // SUB * SUB
    rest = block // HALVES - main
    row_total = sources * (main + HALVES * rest)
    depth, both = rows_weight.shape
    hidden = both // 2
    tile = 256
    steps = hidden // tile
    whole = pl.BlockSpec(arrived.shape, lambda j: (0, 0, 0))
    return pl.pallas_call(
        expert_kernel,
        grid=(steps,),
        out_shape=jax.ShapeDtypeStruct(arrived.shape, jnp.bfloat16),
        in_specs=[
            whole,
            pl.BlockSpec((depth, tile), lambda j: (0, j)),
            pl.BlockSpec((depth, tile), lambda j: (0, steps + j)),
            pl.BlockSpec((tile, depth), lambda j: (j, 0)),
        ],
        out_specs=whole,
        scratch_shapes=[
            pltpu.VMEM((row_total, depth), jnp.bfloat16),
            pltpu.VMEM((row_total, depth), jnp.float32),
        ],
        compiler_params=pltpu.CompilerParams(vmem_limit_bytes=48 * 1024 * 1024),
        cost_estimate=pl.CostEstimate(
            flops=7 * 10**9, bytes_accessed=15 * 10**6, transcendentals=589824
        ),
    )(arrived, rows_weight, rows_weight, cols_weight)


def body(
    new_q,
    new_kv,
    cache_kv,
    cache_len,
    prompt_kv,
    prompt_len,
    residual,
    norm_gain,
    routes,
    route_weight,
    gate_up,
    down_proj,
):
    experts_here = lax.axis_size("exp")
    token_count = new_q.shape[0]
    capacity = token_count * TOP * 5 // (4 * experts_here)
    spread, half, slot = slot_layout(experts_here, capacity)
    chosen = membership(routes, experts_here)
    codes = slot_codes(chosen, spread)
    rows_weight, cols_weight = (
        lax.all_gather(gate_up[0], "req", axis=0, tiled=True),
        lax.all_gather(down_proj[0], "req", axis=1, tiled=True),
    )
    stream, outbox = attend_and_pack(
        new_q,
        new_kv,
        cache_kv,
        cache_len,
        prompt_kv,
        prompt_len,
        residual,
        norm_gain,
        routes,
        experts_here,
        capacity,
    )
    outbox = outbox.reshape(experts_here, HALVES * capacity, -1)
    arrived = lax.all_to_all(outbox, "exp", split_axis=0, concat_axis=0, tiled=True)
    returned = lax.all_to_all(
        expert_local(arrived, rows_weight, cols_weight),
        "exp",
        split_axis=0,
        concat_axis=0,
        tiled=True,
    )
    returned = returned.reshape(-1, returned.shape[-1])
    combined = combine_rows(returned, chosen, route_weight, codes, spread, half, slot)
    return (stream + combined).astype(jnp.bfloat16)


def solution(mesh):
    return jax.shard_map(
        body,
        mesh=mesh,
        in_specs=(
            P(("req", "exp"), None),
            P(("req", "exp"), None),
            P(("req", "exp"), None),
            P(("req", "exp")),
            P(("req", "exp"), None),
            P(("req", "exp")),
            P(("req", "exp"), None),
            P(),
            P(("req", "exp"), None),
            P(("req", "exp"), None),
            P("exp", "req", None),
            P("exp", None, "req"),
        ),
        out_specs=P(("req", "exp"), None),
        check_vma=False,
    )
```

```python
import math

import jax
import jax.numpy as jnp
import numpy as np
from jax import lax
from jax.experimental import pallas as pl
from jax.experimental.pallas import tpu as pltpu
from jax.sharding import PartitionSpec as P

HEADS = 16
HDIM = 128
TOP = 4
GROUP = 8


eps_norm = 1e-06


HALVES = 2
SUB = 8


def slot_layout(expert_count, capacity):
    main = capacity // SUB * SUB
    rest = capacity - main
    block = HALVES * capacity
    row = jnp.arange(expert_count * block, dtype=jnp.int32)
    expert = row // block
    inner = row % block
    in_main = inner < HALVES * main
    left_over = inner - HALVES * main
    half = jnp.where(in_main, inner // main, left_over // rest)
    slot = jnp.where(in_main, inner % main, main + left_over % rest)
    spread = (jnp.arange(expert_count, dtype=jnp.int32)[:, None] == expert[None, :]).astype(
        jnp.bfloat16
    )
    return spread, half, slot


def membership(routes, expert_count):
    experts = jnp.arange(expert_count, dtype=jnp.int32)
    return routes[:, :, None] == experts[None, None, :]


def slot_codes(chosen, spread):
    member = jnp.any(chosen, axis=1)
    tok_count = member.shape[0]
    order = jnp.arange(tok_count, dtype=jnp.int32)
    up_to = (order[None, :] <= order[:, None]).astype(jnp.bfloat16)
    upto_count = jnp.dot(
        up_to, member.astype(jnp.bfloat16), preferred_element_type=jnp.float32
    )
    codes = jnp.where(member, upto_count, 0.0).astype(jnp.bfloat16)
    return jnp.dot(codes, spread, preferred_element_type=jnp.float32).astype(jnp.bfloat16)


def combine_rows(returned, chosen, route_weight, codes, spread, half, slot):
    tok_count = route_weight.shape[0]
    by_expert = jnp.sum(jnp.where(chosen, route_weight[:, :, None], 0.0), axis=1)
    high = by_expert.astype(jnp.bfloat16)
    low = (by_expert - high.astype(jnp.float32)).astype(jnp.bfloat16)
    wide = jnp.dot(
        jnp.concatenate([high, low], axis=0), spread, preferred_element_type=jnp.float32
    ).astype(jnp.bfloat16)
    wanted = (slot + 1).astype(jnp.bfloat16)
    hit = codes == wanted[None, :]
    hits = jnp.concatenate([hit, hit], axis=0)
    mixes = [
        jnp.where((half == which)[None, :] & hits, wide, 0.0).astype(jnp.bfloat16)
        for which in range(HALVES)
    ]
    summed = jnp.dot(
        jnp.concatenate(mixes, axis=0), returned, preferred_element_type=jnp.float32
    )
    pieces = [
        summed[2 * which * tok_count : (2 * which + 1) * tok_count]
        + summed[(2 * which + 1) * tok_count : (2 * which + 2) * tok_count]
        for which in range(HALVES)
    ]
    return jnp.concatenate(pieces, axis=1)


def slot_tables(expert_count, capacity):
    main = capacity // SUB * SUB
    rest = capacity - main
    block = HALVES * capacity
    row = np.arange(expert_count * block)
    inner = row % block
    in_main = inner < HALVES * main
    left_over = inner - HALVES * main
    half = np.where(in_main, inner // main, left_over // rest)
    slot = np.where(in_main, inner % main, main + left_over % rest)
    spread = (np.arange(expert_count)[None, :] == (row // block)[:, None]).astype(np.float32)
    wanted = np.stack(
        [np.where(half == which, slot + 1, -1) for which in range(HALVES)], axis=1
    ).astype(np.float32)
    return spread, wanted


NT = (((1,), (1,)), ((), ()))


def attend_kernel(
    count_ref,
    block_ref,
    routes_ref,
    query_hbm,
    own_hbm,
    cache_hbm,
    residual_hbm,
    gain_hbm,
    spread_hbm,
    wanted_hbm,
    stream_hbm,
    outbox_ref,
    query_ref,
    own_ref,
    cache_ref,
    residual_ref,
    gain_ref,
    spread_ref,
    wanted_ref,
    stream_ref,
    far_ref,
    local_ref,
    load_sem,
    send_sem,
    recv_sem,
):
    loads = []
    for source, target in (
        (query_hbm, query_ref),
        (own_hbm, own_ref),
        (cache_hbm, cache_ref),
        (spread_hbm, spread_ref),
        (wanted_hbm, wanted_ref),
        (residual_hbm, residual_ref),
        (gain_hbm, gain_ref),
    ):
        load = pltpu.make_async_copy(source, target, load_sem.at[len(loads)])
        load.start()
        loads.append(load)
    tok_count, width = query_ref.shape
    heads = width // HDIM
    experts = spread_ref.shape[1]
    position = lax.axis_index("exp")
    base = position // GROUP * GROUP
    rank = position - base
    barrier = pltpu.get_barrier_semaphore()
    for offset in range(1, GROUP):
        pl.semaphore_signal(
            barrier,
            inc=1,
            device_id={"exp": base + (rank + offset) % GROUP},
            device_id_type=pl.DeviceIdType.MESH,
        )
    pl.semaphore_wait(barrier, GROUP - 1)
    copies = []
    for offset in range(1, GROUP):
        copy = pltpu.make_async_remote_copy(
            src_ref=block_ref,
            dst_ref=far_ref.at[offset - 1],
            send_sem=send_sem.at[offset - 1],
            recv_sem=recv_sem.at[offset - 1],
            device_id={"exp": base + (rank + offset) % GROUP},
            device_id_type=pl.DeviceIdType.MESH,
        )
        copy.start()
        copies.append(copy)

    scale = 1.0 / math.sqrt(HDIM)
    rows = lax.broadcasted_iota(jnp.int32, (tok_count, tok_count), 0)
    cols = lax.broadcasted_iota(jnp.int32, (tok_count, tok_count), 1)
    causal = cols <= rows
    live = lax.broadcasted_iota(jnp.int32, (tok_count, cache_ref.shape[0]), 1) < count_ref[0]
    peaks = []
    sums = []
    for load in loads[:3]:
        load.wait()
    for head in range(heads):
        at = slice(head * HDIM, (head + 1) * HDIM)
        values_at = slice(width + head * HDIM, width + (head + 1) * HDIM)
        query = query_ref[:, at]
        own = lax.dot_general(query, own_ref[:, at], NT, preferred_element_type=jnp.float32)
        old = lax.dot_general(query, cache_ref[:, at], NT, preferred_element_type=jnp.float32)
        own = jnp.where(causal, own * scale, -jnp.inf)
        old = jnp.where(live, old * scale, -jnp.inf)
        peak = jnp.max(jnp.maximum(own, old), axis=1, keepdims=True)
        own = jnp.exp(own - peak)
        old = jnp.exp(old - peak)
        sums.append(jnp.sum(own + old, axis=1, keepdims=True))
        peaks.append(peak)
        local_ref[:, at] = jnp.dot(
            own.astype(jnp.bfloat16), own_ref[:, values_at], preferred_element_type=jnp.float32
        ) + jnp.dot(
            old.astype(jnp.bfloat16), cache_ref[:, values_at], preferred_element_type=jnp.float32
        )

    for load in loads[3:]:
        load.wait()
    names = lax.broadcasted_iota(jnp.int32, (experts, tok_count), 0)
    member = jnp.zeros((experts, tok_count), jnp.float32)
    for k in range(TOP):
        member = member + jnp.where(routes_ref[k : k + 1, :] == names, 1.0, 0.0)
    ranks = jnp.dot(
        member.astype(jnp.bfloat16),
        jnp.where(rows <= cols, 1.0, 0.0).astype(jnp.bfloat16),
        preferred_element_type=jnp.float32,
    )
    codes = (ranks * member).astype(jnp.bfloat16)
    codes = jnp.dot(spread_ref[...], codes, preferred_element_type=jnp.float32)
    picks = [
        jnp.where(codes == wanted_ref[:, which : which + 1], 1.0, 0.0).astype(jnp.bfloat16)
        for which in range(HALVES)
    ]

    for copy in copies:
        copy.wait()
    prompt_rows = block_ref.shape[0]
    far = jnp.concatenate([block_ref[...][None], far_ref[...]], axis=0)
    in_segment = lax.broadcasted_iota(jnp.int32, (GROUP, prompt_rows, HDIM), 1)
    dead = jnp.where(
        in_segment.astype(jnp.float32) < far[:, :, 2 * width :].astype(jnp.float32), 0.0, 1.0
    )
    keys_total = GROUP * prompt_rows
    dead = dead.reshape(keys_total, HDIM).astype(jnp.bfloat16)
    far = far.reshape(keys_total, far.shape[2])
    ones = jnp.full((tok_count, HDIM), 1.0 / HDIM, jnp.bfloat16)
    hidden = lax.dot_general(ones, dead, NT, preferred_element_type=jnp.float32) > 0.5
    squares = jnp.zeros((tok_count, HDIM), jnp.float32)
    for head in range(heads):
        at = slice(head * HDIM, (head + 1) * HDIM)
        values_at = slice(width + head * HDIM, width + (head + 1) * HDIM)
        scores = lax.dot_general(
            query_ref[:, at], far[:, at], NT, preferred_element_type=jnp.float32
        )
        scores = jnp.where(hidden, -jnp.inf, scores * scale)
        peak = jnp.maximum(peaks[head], jnp.max(scores, axis=1, keepdims=True))
        shrink = jnp.exp(peaks[head] - peak)
        weights = jnp.exp(scores - peak)
        total = sums[head] * shrink + jnp.sum(weights, axis=1, keepdims=True)
        summed = local_ref[:, at] * shrink + jnp.dot(
            weights.astype(jnp.bfloat16), far[:, values_at], preferred_element_type=jnp.float32
        )
        attended = (summed / total).astype(jnp.bfloat16).astype(jnp.float32)
        stream = residual_ref[:, at].astype(jnp.float32) + attended
        stream_ref[:, at] = stream
        squares = squares + stream * stream
    mean_sq = jnp.sum(squares, axis=1, keepdims=True) / width
    normed = (stream_ref[...] * lax.rsqrt(mean_sq + eps_norm) * gain_ref[...]).astype(jnp.bfloat16)
    store = pltpu.make_async_copy(stream_ref, stream_hbm, load_sem.at[len(loads)])
    store.start()
    part = width // HALVES
    outbox_ref[...] = (
        jnp.dot(picks[0], normed[:, :part], preferred_element_type=jnp.float32)
        + jnp.dot(picks[1], normed[:, part:], preferred_element_type=jnp.float32)
    ).astype(jnp.bfloat16)
    store.wait()


def attend_and_pack(
    query, own_kv, own_cache, cache_count, prompt_kv, prompt_len, residual, gain, routes, experts, capacity
):
    tok_count, width = query.shape
    prompt_rows = prompt_kv.shape[0]
    count_cols = jnp.broadcast_to(prompt_len.astype(jnp.bfloat16)[:, None], (prompt_rows, HDIM))
    block = jnp.concatenate([prompt_kv, count_cols], axis=1)
    spread, wanted = slot_tables(experts, capacity)
    vmem = pl.BlockSpec(memory_space=pltpu.VMEM)
    outside = pl.BlockSpec(memory_space=pltpu.HBM)
    slots = experts * HALVES * capacity
    return pl.pallas_call(
        attend_kernel,
        out_shape=(
            jax.ShapeDtypeStruct((tok_count, width), jnp.float32),
            jax.ShapeDtypeStruct((slots, width // HALVES), jnp.bfloat16),
        ),
        in_specs=[pl.BlockSpec(memory_space=pltpu.SMEM)] + [vmem] * 2 + [outside] * 7,
        out_specs=(outside, vmem),
        scratch_shapes=[
            pltpu.VMEM(query.shape, query.dtype),
            pltpu.VMEM(own_kv.shape, own_kv.dtype),
            pltpu.VMEM(own_cache.shape, own_cache.dtype),
            pltpu.VMEM(residual.shape, residual.dtype),
            pltpu.VMEM((1, width), jnp.float32),
            pltpu.VMEM(spread.shape, jnp.bfloat16),
            pltpu.VMEM(wanted.shape, jnp.float32),
            pltpu.VMEM((tok_count, width), jnp.float32),
            pltpu.VMEM((GROUP - 1,) + block.shape, jnp.bfloat16),
            pltpu.VMEM((tok_count, width), jnp.float32),
            pltpu.SemaphoreType.DMA((8,)),
            pltpu.SemaphoreType.DMA((GROUP - 1,)),
            pltpu.SemaphoreType.DMA((GROUP - 1,)),
        ],
        compiler_params=pltpu.CompilerParams(
            collective_id=0, has_side_effects=True, vmem_limit_bytes=63 * 1024 * 1024
        ),
        cost_estimate=pl.CostEstimate(
            flops=2 * 10**9, bytes_accessed=8 * 10**6, transcendentals=655360
        ),
    )(
        cache_count,
        block,
        routes.T,
        query,
        own_kv,
        own_cache,
        residual,
        gain[None, :],
        jnp.asarray(spread, jnp.bfloat16),
        jnp.asarray(wanted),
    )


def expert_kernel(arrived_ref, gate_ref, up_ref, down_ref, out_ref, rows_ref, total_ref):
    step = pl.program_id(0)
    sources, block, width = arrived_ref.shape
    main = block // HALVES // SUB * SUB
    rest = block // HALVES - main
    tall = sources * main

    @pl.when(step == 0)
    def _():
        rows_ref[:tall, :width] = arrived_ref[:, :main, :].reshape(tall, width)
        rows_ref[:tall, width:] = arrived_ref[:, main : HALVES * main, :].reshape(tall, width)
        tail = arrived_ref[:, HALVES * main :, :].astype(jnp.float32)
        swapped = jnp.concatenate([tail[:, rest:], tail[:, :rest]], axis=1)
        rows_ref[tall:, :width] = tail.reshape(-1, width).astype(jnp.bfloat16)
        rows_ref[tall:, width:] = swapped.reshape(-1, width).astype(jnp.bfloat16)

    rows = rows_ref[...]
    gate = jnp.dot(rows, gate_ref[...], preferred_element_type=jnp.float32)
    up = jnp.dot(rows, up_ref[...], preferred_element_type=jnp.float32)
    activated = (gate / (1.0 + jnp.exp(-gate)) * up).astype(jnp.bfloat16)
    down = jnp.concatenate([down_ref[n] for n in range(down_ref.shape[0])], axis=1)
    result = jnp.dot(activated, down, preferred_element_type=jnp.float32)

    @pl.when(step == 0)
    def _():
        total_ref[...] = result

    @pl.when(step > 0)
    def _():
        total_ref[...] = total_ref[...] + result

    @pl.when(step == pl.num_programs(0) - 1)
    def _():
        out_ref[:, :main, :] = (
            total_ref[:tall, :width].astype(jnp.bfloat16).reshape(sources, main, width)
        )
        out_ref[:, main : HALVES * main, :] = (
            total_ref[:tall, width:].astype(jnp.bfloat16).reshape(sources, main, width)
        )
        left = total_ref[tall:, :width].reshape(sources, HALVES * rest, width)
        right = total_ref[tall:, width:].reshape(sources, HALVES * rest, width)
        out_ref[:, HALVES * main :, :] = jnp.concatenate(
            [left[:, :rest], right[:, :rest]], axis=1
        ).astype(jnp.bfloat16)


def expert_local(arrived, rows_weight, cols_weight):
    sources, block, width = arrived.shape
    main = block // HALVES // SUB * SUB
    rest = block // HALVES - main
    row_total = sources * (main + HALVES * rest)
    depth, both = rows_weight.shape
    hidden = both // 2
    tile = 256
    steps = hidden // tile
    whole = pl.BlockSpec(arrived.shape, lambda j: (0, 0, 0))
    return pl.pallas_call(
        expert_kernel,
        grid=(steps,),
        out_shape=jax.ShapeDtypeStruct(arrived.shape, jnp.bfloat16),
        in_specs=[
            whole,
            pl.BlockSpec((depth, tile), lambda j: (0, j)),
            pl.BlockSpec((depth, tile), lambda j: (0, steps + j)),
            pl.BlockSpec((cols_weight.shape[0], tile, cols_weight.shape[2]), lambda j: (0, j, 0)),
        ],
        out_specs=whole,
        scratch_shapes=[
            pltpu.VMEM((row_total, depth), jnp.bfloat16),
            pltpu.VMEM((row_total, depth), jnp.float32),
        ],
        compiler_params=pltpu.CompilerParams(vmem_limit_bytes=48 * 1024 * 1024),
        cost_estimate=pl.CostEstimate(
            flops=7 * 10**9, bytes_accessed=15 * 10**6, transcendentals=589824
        ),
    )(arrived, rows_weight, rows_weight, cols_weight)


def body(
    new_q,
    new_kv,
    cache_kv,
    cache_len,
    prompt_kv,
    prompt_len,
    residual,
    norm_gain,
    routes,
    route_weight,
    gate_up,
    down_proj,
):
    experts_here = lax.axis_size("exp")
    token_count = new_q.shape[0]
    capacity = token_count * TOP * 5 // (4 * experts_here)
    spread, half, slot = slot_layout(experts_here, capacity)
    chosen = membership(routes, experts_here)
    codes = slot_codes(chosen, spread)
    rows_weight, cols_weight = (
        lax.all_gather(gate_up[0], "req", axis=0, tiled=True),
        lax.all_gather(down_proj, "req", axis=0, tiled=True),
    )
    stream, outbox = attend_and_pack(
        new_q,
        new_kv,
        cache_kv,
        cache_len,
        prompt_kv,
        prompt_len,
        residual,
        norm_gain,
        routes,
        experts_here,
        capacity,
    )
    outbox = outbox.reshape(experts_here, HALVES * capacity, -1)
    arrived = lax.all_to_all(outbox, "exp", split_axis=0, concat_axis=0, tiled=True)
    returned = lax.all_to_all(
        expert_local(arrived, rows_weight, cols_weight),
        "exp",
        split_axis=0,
        concat_axis=0,
        tiled=True,
    )
    returned = returned.reshape(-1, returned.shape[-1])
    combined = combine_rows(returned, chosen, route_weight, codes, spread, half, slot)
    return (stream + combined).astype(jnp.bfloat16)


def solution(mesh):
    return jax.shard_map(
        body,
        mesh=mesh,
        in_specs=(
            P(("req", "exp"), None),
            P(("req", "exp"), None),
            P(("req", "exp"), None),
            P(("req", "exp")),
            P(("req", "exp"), None),
            P(("req", "exp")),
            P(("req", "exp"), None),
            P(),
            P(("req", "exp"), None),
            P(("req", "exp"), None),
            P("exp", "req", None),
            P("exp", None, "req"),
        ),
        out_specs=P(("req", "exp"), None),
        check_vma=False,
    )
```

```python
import math

import jax
import jax.numpy as jnp
import numpy as np
from jax import lax
from jax.experimental import pallas as pl
from jax.experimental.pallas import tpu as pltpu
from jax.sharding import PartitionSpec as P

HEADS = 16
HDIM = 128
TOP = 4
GROUP = 8


eps_norm = 1e-06


HALVES = 2
SUB = 8
ACROSS = 4


def slot_layout(expert_count, capacity):
    main = capacity // SUB * SUB
    rest = capacity - main
    block = HALVES * capacity
    row = jnp.arange(expert_count * block, dtype=jnp.int32)
    expert = row // block
    inner = row % block
    in_main = inner < HALVES * main
    left_over = inner - HALVES * main
    half = jnp.where(in_main, inner // main, left_over // rest)
    slot = jnp.where(in_main, inner % main, main + left_over % rest)
    spread = (jnp.arange(expert_count, dtype=jnp.int32)[:, None] == expert[None, :]).astype(
        jnp.bfloat16
    )
    return spread, half, slot


def membership(routes, expert_count):
    experts = jnp.arange(expert_count, dtype=jnp.int32)
    return routes[:, :, None] == experts[None, None, :]


def slot_codes(chosen, spread):
    member = jnp.any(chosen, axis=1)
    tok_count = member.shape[0]
    order = jnp.arange(tok_count, dtype=jnp.int32)
    up_to = (order[None, :] <= order[:, None]).astype(jnp.bfloat16)
    upto_count = jnp.dot(
        up_to, member.astype(jnp.bfloat16), preferred_element_type=jnp.float32
    )
    codes = jnp.where(member, upto_count, 0.0).astype(jnp.bfloat16)
    return jnp.dot(codes, spread, preferred_element_type=jnp.float32).astype(jnp.bfloat16)


def combine_rows(returned, chosen, route_weight, codes, spread, half, slot):
    tok_count = route_weight.shape[0]
    by_expert = jnp.sum(jnp.where(chosen, route_weight[:, :, None], 0.0), axis=1)
    high = by_expert.astype(jnp.bfloat16)
    low = (by_expert - high.astype(jnp.float32)).astype(jnp.bfloat16)
    wide = jnp.dot(
        jnp.concatenate([high, low], axis=0), spread, preferred_element_type=jnp.float32
    ).astype(jnp.bfloat16)
    wanted = (slot + 1).astype(jnp.bfloat16)
    hit = codes == wanted[None, :]
    hits = jnp.concatenate([hit, hit], axis=0)
    mixes = [
        jnp.where((half == which)[None, :] & hits, wide, 0.0).astype(jnp.bfloat16)
        for which in range(HALVES)
    ]
    summed = jnp.dot(
        jnp.concatenate(mixes, axis=0), returned, preferred_element_type=jnp.float32
    )
    pieces = [
        summed[2 * which * tok_count : (2 * which + 1) * tok_count]
        + summed[(2 * which + 1) * tok_count : (2 * which + 2) * tok_count]
        for which in range(HALVES)
    ]
    return jnp.concatenate(pieces, axis=1)


def slot_tables(expert_count, capacity):
    main = capacity // SUB * SUB
    rest = capacity - main
    block = HALVES * capacity
    row = np.arange(expert_count * block)
    inner = row % block
    in_main = inner < HALVES * main
    left_over = inner - HALVES * main
    half = np.where(in_main, inner // main, left_over // rest)
    slot = np.where(in_main, inner % main, main + left_over % rest)
    spread = (np.arange(expert_count)[None, :] == (row // block)[:, None]).astype(np.float32)
    wanted = np.stack(
        [np.where(half == which, slot + 1, -1) for which in range(HALVES)], axis=1
    ).astype(np.float32)
    return spread, wanted


NT = (((1,), (1,)), ((), ()))


def attend_kernel(
    count_ref,
    block_ref,
    routes_ref,
    query_hbm,
    own_hbm,
    cache_hbm,
    residual_hbm,
    gain_hbm,
    spread_hbm,
    wanted_hbm,
    stream_hbm,
    outbox_ref,
    query_ref,
    own_ref,
    cache_ref,
    residual_ref,
    gain_ref,
    spread_ref,
    wanted_ref,
    stream_ref,
    far_ref,
    local_ref,
    load_sem,
    send_sem,
    recv_sem,
):
    loads = []
    for source, target in (
        (query_hbm, query_ref),
        (own_hbm, own_ref),
        (cache_hbm, cache_ref),
        (spread_hbm, spread_ref),
        (wanted_hbm, wanted_ref),
        (residual_hbm, residual_ref),
        (gain_hbm, gain_ref),
    ):
        load = pltpu.make_async_copy(source, target, load_sem.at[len(loads)])
        load.start()
        loads.append(load)
    tok_count, width = query_ref.shape
    heads = width // HDIM
    experts = spread_ref.shape[1]
    position = lax.axis_index("exp")
    base = position // GROUP * GROUP
    rank = position - base
    barrier = pltpu.get_barrier_semaphore()
    for offset in range(1, GROUP):
        pl.semaphore_signal(
            barrier,
            inc=1,
            device_id={"exp": base + (rank + offset) % GROUP},
            device_id_type=pl.DeviceIdType.MESH,
        )
    pl.semaphore_wait(barrier, GROUP - 1)
    copies = []
    for offset in range(1, GROUP):
        copy = pltpu.make_async_remote_copy(
            src_ref=block_ref,
            dst_ref=far_ref.at[offset - 1],
            send_sem=send_sem.at[offset - 1],
            recv_sem=recv_sem.at[offset - 1],
            device_id={"exp": base + (rank + offset) % GROUP},
            device_id_type=pl.DeviceIdType.MESH,
        )
        copy.start()
        copies.append(copy)

    scale = 1.0 / math.sqrt(HDIM)
    rows = lax.broadcasted_iota(jnp.int32, (tok_count, tok_count), 0)
    cols = lax.broadcasted_iota(jnp.int32, (tok_count, tok_count), 1)
    causal = cols <= rows
    live = lax.broadcasted_iota(jnp.int32, (tok_count, cache_ref.shape[0]), 1) < count_ref[0]
    peaks = []
    sums = []
    for load in loads[:3]:
        load.wait()
    for head in range(heads):
        at = slice(head * HDIM, (head + 1) * HDIM)
        values_at = slice(width + head * HDIM, width + (head + 1) * HDIM)
        query = query_ref[:, at]
        own = lax.dot_general(query, own_ref[:, at], NT, preferred_element_type=jnp.float32)
        old = lax.dot_general(query, cache_ref[:, at], NT, preferred_element_type=jnp.float32)
        own = jnp.where(causal, own * scale, -jnp.inf)
        old = jnp.where(live, old * scale, -jnp.inf)
        peak = jnp.max(jnp.maximum(own, old), axis=1, keepdims=True)
        own = jnp.exp(own - peak)
        old = jnp.exp(old - peak)
        sums.append(jnp.sum(own + old, axis=1, keepdims=True))
        peaks.append(peak)
        local_ref[:, at] = jnp.dot(
            own.astype(jnp.bfloat16), own_ref[:, values_at], preferred_element_type=jnp.float32
        ) + jnp.dot(
            old.astype(jnp.bfloat16), cache_ref[:, values_at], preferred_element_type=jnp.float32
        )

    for load in loads[3:]:
        load.wait()
    names = lax.broadcasted_iota(jnp.int32, (experts, tok_count), 0)
    member = jnp.zeros((experts, tok_count), jnp.float32)
    for k in range(TOP):
        member = member + jnp.where(routes_ref[k : k + 1, :] == names, 1.0, 0.0)
    ranks = jnp.dot(
        member.astype(jnp.bfloat16),
        jnp.where(rows <= cols, 1.0, 0.0).astype(jnp.bfloat16),
        preferred_element_type=jnp.float32,
    )
    codes = (ranks * member).astype(jnp.bfloat16)
    codes = jnp.dot(spread_ref[...], codes, preferred_element_type=jnp.float32)
    picks = [
        jnp.where(codes == wanted_ref[:, which : which + 1], 1.0, 0.0).astype(jnp.bfloat16)
        for which in range(HALVES)
    ]

    for copy in copies:
        copy.wait()
    prompt_rows = block_ref.shape[0]
    far = jnp.concatenate([block_ref[...][None], far_ref[...]], axis=0)
    in_segment = lax.broadcasted_iota(jnp.int32, (GROUP, prompt_rows, HDIM), 1)
    dead = jnp.where(
        in_segment.astype(jnp.float32) < far[:, :, 2 * width :].astype(jnp.float32), 0.0, 1.0
    )
    keys_total = GROUP * prompt_rows
    dead = dead.reshape(keys_total, HDIM).astype(jnp.bfloat16)
    far = far.reshape(keys_total, far.shape[2])
    ones = jnp.full((tok_count, HDIM), 1.0 / HDIM, jnp.bfloat16)
    hidden = lax.dot_general(ones, dead, NT, preferred_element_type=jnp.float32) > 0.5
    squares = jnp.zeros((tok_count, HDIM), jnp.float32)
    for head in range(heads):
        at = slice(head * HDIM, (head + 1) * HDIM)
        values_at = slice(width + head * HDIM, width + (head + 1) * HDIM)
        scores = lax.dot_general(
            query_ref[:, at], far[:, at], NT, preferred_element_type=jnp.float32
        )
        scores = jnp.where(hidden, -jnp.inf, scores * scale)
        peak = jnp.maximum(peaks[head], jnp.max(scores, axis=1, keepdims=True))
        shrink = jnp.exp(peaks[head] - peak)
        weights = jnp.exp(scores - peak)
        total = sums[head] * shrink + jnp.sum(weights, axis=1, keepdims=True)
        summed = local_ref[:, at] * shrink + jnp.dot(
            weights.astype(jnp.bfloat16), far[:, values_at], preferred_element_type=jnp.float32
        )
        attended = (summed / total).astype(jnp.bfloat16).astype(jnp.float32)
        stream = residual_ref[:, at].astype(jnp.float32) + attended
        stream_ref[:, at] = stream
        squares = squares + stream * stream
    mean_sq = jnp.sum(squares, axis=1, keepdims=True) / width
    normed = (stream_ref[...] * lax.rsqrt(mean_sq + eps_norm) * gain_ref[...]).astype(jnp.bfloat16)
    store = pltpu.make_async_copy(stream_ref, stream_hbm, load_sem.at[len(loads)])
    store.start()
    part = width // HALVES
    outbox_ref[...] = (
        jnp.dot(picks[0], normed[:, :part], preferred_element_type=jnp.float32)
        + jnp.dot(picks[1], normed[:, part:], preferred_element_type=jnp.float32)
    ).astype(jnp.bfloat16)
    store.wait()


def attend_and_pack(
    query, own_kv, own_cache, cache_count, prompt_kv, prompt_len, residual, gain, routes, experts, capacity
):
    tok_count, width = query.shape
    prompt_rows = prompt_kv.shape[0]
    count_cols = jnp.broadcast_to(prompt_len.astype(jnp.bfloat16)[:, None], (prompt_rows, HDIM))
    block = jnp.concatenate([prompt_kv, count_cols], axis=1)
    spread, wanted = slot_tables(experts, capacity)
    vmem = pl.BlockSpec(memory_space=pltpu.VMEM)
    outside = pl.BlockSpec(memory_space=pltpu.HBM)
    slots = experts * HALVES * capacity
    return pl.pallas_call(
        attend_kernel,
        out_shape=(
            jax.ShapeDtypeStruct((tok_count, width), jnp.float32),
            jax.ShapeDtypeStruct((slots, width // HALVES), jnp.bfloat16),
        ),
        in_specs=[pl.BlockSpec(memory_space=pltpu.SMEM)] + [vmem] * 2 + [outside] * 7,
        out_specs=(outside, vmem),
        scratch_shapes=[
            pltpu.VMEM(query.shape, query.dtype),
            pltpu.VMEM(own_kv.shape, own_kv.dtype),
            pltpu.VMEM(own_cache.shape, own_cache.dtype),
            pltpu.VMEM(residual.shape, residual.dtype),
            pltpu.VMEM((1, width), jnp.float32),
            pltpu.VMEM(spread.shape, jnp.bfloat16),
            pltpu.VMEM(wanted.shape, jnp.float32),
            pltpu.VMEM((tok_count, width), jnp.float32),
            pltpu.VMEM((GROUP - 1,) + block.shape, jnp.bfloat16),
            pltpu.VMEM((tok_count, width), jnp.float32),
            pltpu.SemaphoreType.DMA((8,)),
            pltpu.SemaphoreType.DMA((GROUP - 1,)),
            pltpu.SemaphoreType.DMA((GROUP - 1,)),
        ],
        compiler_params=pltpu.CompilerParams(
            collective_id=0, has_side_effects=True, vmem_limit_bytes=63 * 1024 * 1024
        ),
        cost_estimate=pl.CostEstimate(
            flops=2 * 10**9, bytes_accessed=8 * 10**6, transcendentals=655360
        ),
    )(
        cache_count,
        block,
        routes.T,
        query,
        own_kv,
        own_cache,
        residual,
        gain[None, :],
        jnp.asarray(spread, jnp.bfloat16),
        jnp.asarray(wanted),
    )


def pack_weights(gate_up, down_proj):
    hidden = down_proj.shape[0]
    pieces = gate_up.shape[1] // HDIM
    tall = hidden // pieces
    folded = jnp.concatenate(
        [down_proj[one * tall : (one + 1) * tall] for one in range(pieces)], axis=1
    )
    return jnp.concatenate([gate_up, folded], axis=0)


def expert_kernel(
    arrived_ref,
    weight_hbm,
    out_ref,
    weight_ref,
    rows_ref,
    total_ref,
    sent_ref,
    load_sem,
    send_sem,
    recv_sem,
):
    layers, across, block, width = arrived_ref.shape
    shards, _, both = weight_ref.shape
    hidden = both // 2
    depth = HALVES * width // shards
    fold = hidden * HDIM // both
    tile = 2 * HDIM
    main = block // HALVES // SUB * SUB
    rest = block // HALVES - main
    pair = 2
    tall = layers * main
    low = layers * HALVES * rest
    me = lax.axis_index("exp")
    my_layer = me // across
    my_place = me % across
    loads = []
    for part in range(4):
        span = slice(part * shards // 4, (part + 1) * shards // 4)
        load = pltpu.make_async_copy(weight_hbm.at[span], weight_ref.at[span], load_sem.at[part])
        load.start()
        loads.append(load)
    barrier = pltpu.get_barrier_semaphore()
    for offset in range(1, layers * across):
        pl.semaphore_signal(
            barrier,
            inc=1,
            device_id={"exp": (me + offset) % (layers * across)},
            device_id_type=pl.DeviceIdType.MESH,
        )
    copies = []
    for chunk in range(across // pair):
        for one in range(pair):
            place = (my_place + chunk * pair + one) % across
            top = slice(one * tall, (one + 1) * tall)
            end = slice(pair * tall + one * low, pair * tall + (one + 1) * low)
            rows_ref[top, :width] = arrived_ref[:, place, :main, :].reshape(tall, width)
            rows_ref[top, width:] = arrived_ref[:, place, main : HALVES * main, :].reshape(
                tall, width
            )
            tail = arrived_ref[:, place, HALVES * main :, :].astype(jnp.float32)
            swapped = jnp.concatenate([tail[:, rest:], tail[:, :rest]], axis=1)
            rows_ref[end, :width] = tail.reshape(low, width).astype(jnp.bfloat16)
            rows_ref[end, width:] = swapped.reshape(low, width).astype(jnp.bfloat16)
        if chunk == 0:
            for load in loads:
                load.wait()
        rows = rows_ref[...]
        for step in range(hidden // tile):
            at = step * tile
            gate_weight = weight_ref[:, :depth, at : at + tile]
            up_weight = weight_ref[:, :depth, hidden + at : hidden + at + tile]
            gate = jnp.dot(
                rows, gate_weight.reshape(shards * depth, tile), preferred_element_type=jnp.float32
            )
            up = jnp.dot(
                rows, up_weight.reshape(shards * depth, tile), preferred_element_type=jnp.float32
            )
            activated = (gate / (1.0 + jnp.exp(-gate)) * up).astype(jnp.bfloat16)
            first = at // fold
            down = jnp.concatenate(
                [
                    jnp.concatenate(
                        [
                            weight_ref[shard, depth:, piece * HDIM : (piece + 1) * HDIM]
                            for piece in range(first, first + tile // fold)
                        ],
                        axis=0,
                    )
                    for shard in range(shards)
                ],
                axis=1,
            )
            result = jnp.dot(activated, down, preferred_element_type=jnp.float32)
            if step == 0:
                total_ref[...] = result
            else:
                total_ref[...] = total_ref[...] + result
        for one in range(pair):
            turn = chunk * pair + one
            top = slice(one * tall, (one + 1) * tall)
            end = slice(pair * tall + one * low, pair * tall + (one + 1) * low)
            sent_ref[turn, :, :main, :] = (
                total_ref[top, :width].astype(jnp.bfloat16).reshape(layers, main, width)
            )
            sent_ref[turn, :, main : HALVES * main, :] = (
                total_ref[top, width:].astype(jnp.bfloat16).reshape(layers, main, width)
            )
            left = total_ref[end, :width].reshape(layers, HALVES * rest, width)
            right = total_ref[end, width:].reshape(layers, HALVES * rest, width)
            sent_ref[turn, :, HALVES * main :, :] = jnp.concatenate(
                [left[:, :rest], right[:, :rest]], axis=1
            ).astype(jnp.bfloat16)
        if chunk == 0:
            pl.semaphore_wait(barrier, layers * across - 1)
        far_first = sorted(range(layers), key=lambda hop: -min(hop, layers - hop))
        for hop in far_first:
            for one in range(pair):
                turn = chunk * pair + one
                place = (my_place + turn) % across
                layer = (my_layer + hop) % layers
                if turn == 0 and hop == 0:
                    copy = pltpu.make_async_copy(
                        sent_ref.at[turn, layer], out_ref.at[me], load_sem.at[4]
                    )
                else:
                    copy = pltpu.make_async_remote_copy(
                        src_ref=sent_ref.at[turn, layer],
                        dst_ref=out_ref.at[me],
                        send_sem=send_sem.at[turn, hop],
                        recv_sem=recv_sem.at[turn, hop],
                        device_id={"exp": layer * across + place},
                        device_id_type=pl.DeviceIdType.MESH,
                    )
                copy.start()
                copies.append(copy)
    for copy in copies:
        copy.wait()


def expert_and_return(arrived, weights, across):
    sources, block, width = arrived.shape
    layers = sources // across
    both = weights.shape[2]
    row_total = sources // across * 2 * (block // HALVES + block // HALVES % SUB)
    outside = pl.BlockSpec(memory_space=pltpu.HBM)
    return pl.pallas_call(
        expert_kernel,
        out_shape=jax.ShapeDtypeStruct(arrived.shape, jnp.bfloat16),
        in_specs=[pl.BlockSpec(memory_space=pltpu.VMEM), outside],
        out_specs=outside,
        scratch_shapes=[
            pltpu.VMEM(weights.shape, jnp.bfloat16),
            pltpu.VMEM((row_total, HALVES * width), jnp.bfloat16),
            pltpu.VMEM((row_total, HALVES * width), jnp.float32),
            pltpu.VMEM((across, layers, block, width), jnp.bfloat16),
            pltpu.SemaphoreType.DMA((5,)),
            pltpu.SemaphoreType.DMA((across, layers)),
            pltpu.SemaphoreType.DMA((across, layers)),
        ],
        compiler_params=pltpu.CompilerParams(
            collective_id=1, has_side_effects=True, vmem_limit_bytes=56 * 1024 * 1024
        ),
        cost_estimate=pl.CostEstimate(
            flops=7 * 10**9, bytes_accessed=15 * 10**6, transcendentals=589824
        ),
    )(arrived.reshape(layers, across, block, width), weights)


def body(
    new_q,
    new_kv,
    cache_kv,
    cache_len,
    prompt_kv,
    prompt_len,
    residual,
    norm_gain,
    routes,
    route_weight,
    gate_up,
    down_proj,
):
    experts_here = lax.axis_size("exp")
    token_count = new_q.shape[0]
    capacity = token_count * TOP * 5 // (4 * experts_here)
    spread, half, slot = slot_layout(experts_here, capacity)
    chosen = membership(routes, experts_here)
    codes = slot_codes(chosen, spread)
    weights = lax.all_gather(pack_weights(gate_up[0], down_proj[0]), "req", axis=0)
    stream, outbox = attend_and_pack(
        new_q,
        new_kv,
        cache_kv,
        cache_len,
        prompt_kv,
        prompt_len,
        residual,
        norm_gain,
        routes,
        experts_here,
        capacity,
    )
    outbox = outbox.reshape(experts_here, HALVES * capacity, -1)
    arrived = lax.all_to_all(outbox, "exp", split_axis=0, concat_axis=0, tiled=True)
    returned = expert_and_return(arrived, weights, ACROSS)
    returned = returned.reshape(-1, returned.shape[-1])
    combined = combine_rows(returned, chosen, route_weight, codes, spread, half, slot)
    return (stream + combined).astype(jnp.bfloat16)


def solution(mesh):
    return jax.shard_map(
        body,
        mesh=mesh,
        in_specs=(
            P(("req", "exp"), None),
            P(("req", "exp"), None),
            P(("req", "exp"), None),
            P(("req", "exp")),
            P(("req", "exp"), None),
            P(("req", "exp")),
            P(("req", "exp"), None),
            P(),
            P(("req", "exp"), None),
            P(("req", "exp"), None),
            P("exp", "req", None),
            P("exp", None, "req"),
        ),
        out_specs=P(("req", "exp"), None),
        check_vma=False,
    )
```

```python
import math

import jax
import jax.numpy as jnp
import numpy as np
from jax import lax
from jax.experimental import pallas as pl
from jax.experimental.pallas import tpu as pltpu
from jax.sharding import PartitionSpec as P

HEADS = 16
HDIM = 128
TOP = 4
GROUP = 8


eps_norm = 1e-06


HALVES = 2
SUB = 8
ACROSS = 4


def slot_layout(expert_count, capacity):
    main = capacity // SUB * SUB
    rest = capacity - main
    block = HALVES * capacity
    row = jnp.arange(expert_count * block, dtype=jnp.int32)
    expert = row // block
    inner = row % block
    in_main = inner < HALVES * main
    left_over = inner - HALVES * main
    half = jnp.where(in_main, inner // main, left_over // rest)
    slot = jnp.where(in_main, inner % main, main + left_over % rest)
    spread = (jnp.arange(expert_count, dtype=jnp.int32)[:, None] == expert[None, :]).astype(
        jnp.bfloat16
    )
    return spread, half, slot


def membership(routes, expert_count):
    experts = jnp.arange(expert_count, dtype=jnp.int32)
    return routes[:, :, None] == experts[None, None, :]


def slot_codes(chosen, spread):
    member = jnp.any(chosen, axis=1)
    tok_count = member.shape[0]
    order = jnp.arange(tok_count, dtype=jnp.int32)
    up_to = (order[None, :] <= order[:, None]).astype(jnp.bfloat16)
    upto_count = jnp.dot(
        up_to, member.astype(jnp.bfloat16), preferred_element_type=jnp.float32
    )
    codes = jnp.where(member, upto_count, 0.0).astype(jnp.bfloat16)
    return jnp.dot(codes, spread, preferred_element_type=jnp.float32).astype(jnp.bfloat16)


def combine_rows(returned, chosen, route_weight, codes, spread, half, slot):
    tok_count = route_weight.shape[0]
    by_expert = jnp.sum(jnp.where(chosen, route_weight[:, :, None], 0.0), axis=1)
    high = by_expert.astype(jnp.bfloat16)
    low = (by_expert - high.astype(jnp.float32)).astype(jnp.bfloat16)
    wide = jnp.dot(
        jnp.concatenate([high, low], axis=0), spread, preferred_element_type=jnp.float32
    ).astype(jnp.bfloat16)
    wanted = (slot + 1).astype(jnp.bfloat16)
    hit = codes == wanted[None, :]
    hits = jnp.concatenate([hit, hit], axis=0)
    mixes = [
        jnp.where((half == which)[None, :] & hits, wide, 0.0).astype(jnp.bfloat16)
        for which in range(HALVES)
    ]
    summed = jnp.dot(
        jnp.concatenate(mixes, axis=0), returned, preferred_element_type=jnp.float32
    )
    pieces = [
        summed[2 * which * tok_count : (2 * which + 1) * tok_count]
        + summed[(2 * which + 1) * tok_count : (2 * which + 2) * tok_count]
        for which in range(HALVES)
    ]
    return jnp.concatenate(pieces, axis=1)


def slot_tables(expert_count, capacity):
    main = capacity // SUB * SUB
    rest = capacity - main
    block = HALVES * capacity
    row = np.arange(expert_count * block)
    inner = row % block
    in_main = inner < HALVES * main
    left_over = inner - HALVES * main
    half = np.where(in_main, inner // main, left_over // rest)
    slot = np.where(in_main, inner % main, main + left_over % rest)
    spread = (np.arange(expert_count)[None, :] == (row // block)[:, None]).astype(np.float32)
    wanted = np.stack(
        [np.where(half == which, slot + 1, -1) for which in range(HALVES)], axis=1
    ).astype(np.float32)
    return spread, wanted


NT = (((1,), (1,)), ((), ()))


def attend_kernel(
    count_ref,
    block_ref,
    routes_ref,
    query_hbm,
    own_hbm,
    cache_hbm,
    residual_hbm,
    gain_hbm,
    spread_hbm,
    wanted_hbm,
    stream_hbm,
    outbox_ref,
    query_ref,
    own_ref,
    cache_ref,
    residual_ref,
    gain_ref,
    spread_ref,
    wanted_ref,
    stream_ref,
    far_ref,
    local_ref,
    load_sem,
    send_sem,
    recv_sem,
):
    loads = []
    for source, target in (
        (query_hbm, query_ref),
        (own_hbm, own_ref),
        (cache_hbm, cache_ref),
        (spread_hbm, spread_ref),
        (wanted_hbm, wanted_ref),
        (residual_hbm, residual_ref),
        (gain_hbm, gain_ref),
    ):
        load = pltpu.make_async_copy(source, target, load_sem.at[len(loads)])
        load.start()
        loads.append(load)
    tok_count, width = query_ref.shape
    heads = width // HDIM
    experts = spread_ref.shape[1]
    position = lax.axis_index("exp")
    base = position // GROUP * GROUP
    rank = position - base
    barrier = pltpu.get_barrier_semaphore()
    for offset in range(1, GROUP):
        pl.semaphore_signal(
            barrier,
            inc=1,
            device_id={"exp": base + (rank + offset) % GROUP},
            device_id_type=pl.DeviceIdType.MESH,
        )
    pl.semaphore_wait(barrier, GROUP - 1)
    copies = []
    for offset in range(1, GROUP):
        copy = pltpu.make_async_remote_copy(
            src_ref=block_ref,
            dst_ref=far_ref.at[offset - 1],
            send_sem=send_sem.at[offset - 1],
            recv_sem=recv_sem.at[offset - 1],
            device_id={"exp": base + (rank + offset) % GROUP},
            device_id_type=pl.DeviceIdType.MESH,
        )
        copy.start()
        copies.append(copy)

    scale = 1.0 / math.sqrt(HDIM)
    rows = lax.broadcasted_iota(jnp.int32, (tok_count, tok_count), 0)
    cols = lax.broadcasted_iota(jnp.int32, (tok_count, tok_count), 1)
    causal = cols <= rows
    live = lax.broadcasted_iota(jnp.int32, (tok_count, cache_ref.shape[0]), 1) < count_ref[0]
    peaks = []
    sums = []
    for load in loads[:3]:
        load.wait()
    for head in range(heads):
        at = slice(head * HDIM, (head + 1) * HDIM)
        values_at = slice(width + head * HDIM, width + (head + 1) * HDIM)
        query = query_ref[:, at]
        own = lax.dot_general(query, own_ref[:, at], NT, preferred_element_type=jnp.float32)
        old = lax.dot_general(query, cache_ref[:, at], NT, preferred_element_type=jnp.float32)
        own = jnp.where(causal, own * scale, -jnp.inf)
        old = jnp.where(live, old * scale, -jnp.inf)
        peak = jnp.max(jnp.maximum(own, old), axis=1, keepdims=True)
        own = jnp.exp(own - peak)
        old = jnp.exp(old - peak)
        sums.append(jnp.sum(own + old, axis=1, keepdims=True))
        peaks.append(peak)
        local_ref[:, at] = jnp.dot(
            own.astype(jnp.bfloat16), own_ref[:, values_at], preferred_element_type=jnp.float32
        ) + jnp.dot(
            old.astype(jnp.bfloat16), cache_ref[:, values_at], preferred_element_type=jnp.float32
        )

    for load in loads[3:]:
        load.wait()
    names = lax.broadcasted_iota(jnp.int32, (experts, tok_count), 0)
    member = jnp.zeros((experts, tok_count), jnp.float32)
    for k in range(TOP):
        member = member + jnp.where(routes_ref[k : k + 1, :] == names, 1.0, 0.0)
    ranks = jnp.dot(
        member.astype(jnp.bfloat16),
        jnp.where(rows <= cols, 1.0, 0.0).astype(jnp.bfloat16),
        preferred_element_type=jnp.float32,
    )
    codes = (ranks * member).astype(jnp.bfloat16)
    codes = jnp.dot(spread_ref[...], codes, preferred_element_type=jnp.float32)
    picks = [
        jnp.where(codes == wanted_ref[:, which : which + 1], 1.0, 0.0).astype(jnp.bfloat16)
        for which in range(HALVES)
    ]

    for copy in copies:
        copy.wait()
    prompt_rows = block_ref.shape[0]
    far = jnp.concatenate([block_ref[...][None], far_ref[...]], axis=0)
    in_segment = lax.broadcasted_iota(jnp.int32, (GROUP, prompt_rows, HDIM), 1)
    dead = jnp.where(
        in_segment.astype(jnp.float32) < far[:, :, 2 * width :].astype(jnp.float32), 0.0, 1.0
    )
    keys_total = GROUP * prompt_rows
    dead = dead.reshape(keys_total, HDIM).astype(jnp.bfloat16)
    far = far.reshape(keys_total, far.shape[2])
    ones = jnp.full((tok_count, HDIM), 1.0 / HDIM, jnp.bfloat16)
    hidden = lax.dot_general(ones, dead, NT, preferred_element_type=jnp.float32) > 0.5
    squares = jnp.zeros((tok_count, HDIM), jnp.float32)
    for head in range(heads):
        at = slice(head * HDIM, (head + 1) * HDIM)
        values_at = slice(width + head * HDIM, width + (head + 1) * HDIM)
        scores = lax.dot_general(
            query_ref[:, at], far[:, at], NT, preferred_element_type=jnp.float32
        )
        scores = jnp.where(hidden, -jnp.inf, scores * scale)
        peak = jnp.maximum(peaks[head], jnp.max(scores, axis=1, keepdims=True))
        shrink = jnp.exp(peaks[head] - peak)
        weights = jnp.exp(scores - peak)
        total = sums[head] * shrink + jnp.sum(weights, axis=1, keepdims=True)
        summed = local_ref[:, at] * shrink + jnp.dot(
            weights.astype(jnp.bfloat16), far[:, values_at], preferred_element_type=jnp.float32
        )
        attended = (summed / total).astype(jnp.bfloat16).astype(jnp.float32)
        stream = residual_ref[:, at].astype(jnp.float32) + attended
        stream_ref[:, at] = stream
        squares = squares + stream * stream
    mean_sq = jnp.sum(squares, axis=1, keepdims=True) / width
    normed = (stream_ref[...] * lax.rsqrt(mean_sq + eps_norm) * gain_ref[...]).astype(jnp.bfloat16)
    store = pltpu.make_async_copy(stream_ref, stream_hbm, load_sem.at[len(loads)])
    store.start()
    part = width // HALVES
    outbox_ref[...] = (
        jnp.dot(picks[0], normed[:, :part], preferred_element_type=jnp.float32)
        + jnp.dot(picks[1], normed[:, part:], preferred_element_type=jnp.float32)
    ).astype(jnp.bfloat16)
    store.wait()


def attend_and_pack(
    query, own_kv, own_cache, cache_count, prompt_kv, prompt_len, residual, gain, routes, experts, capacity
):
    tok_count, width = query.shape
    prompt_rows = prompt_kv.shape[0]
    count_cols = jnp.broadcast_to(prompt_len.astype(jnp.bfloat16)[:, None], (prompt_rows, HDIM))
    block = jnp.concatenate([prompt_kv, count_cols], axis=1)
    spread, wanted = slot_tables(experts, capacity)
    vmem = pl.BlockSpec(memory_space=pltpu.VMEM)
    outside = pl.BlockSpec(memory_space=pltpu.HBM)
    slots = experts * HALVES * capacity
    return pl.pallas_call(
        attend_kernel,
        out_shape=(
            jax.ShapeDtypeStruct((tok_count, width), jnp.float32),
            jax.ShapeDtypeStruct((slots, width // HALVES), jnp.bfloat16),
        ),
        in_specs=[pl.BlockSpec(memory_space=pltpu.SMEM)] + [vmem] * 2 + [outside] * 7,
        out_specs=(outside, vmem),
        scratch_shapes=[
            pltpu.VMEM(query.shape, query.dtype),
            pltpu.VMEM(own_kv.shape, own_kv.dtype),
            pltpu.VMEM(own_cache.shape, own_cache.dtype),
            pltpu.VMEM(residual.shape, residual.dtype),
            pltpu.VMEM((1, width), jnp.float32),
            pltpu.VMEM(spread.shape, jnp.bfloat16),
            pltpu.VMEM(wanted.shape, jnp.float32),
            pltpu.VMEM((tok_count, width), jnp.float32),
            pltpu.VMEM((GROUP - 1,) + block.shape, jnp.bfloat16),
            pltpu.VMEM((tok_count, width), jnp.float32),
            pltpu.SemaphoreType.DMA((8,)),
            pltpu.SemaphoreType.DMA((GROUP - 1,)),
            pltpu.SemaphoreType.DMA((GROUP - 1,)),
        ],
        compiler_params=pltpu.CompilerParams(
            collective_id=0, has_side_effects=True, vmem_limit_bytes=63 * 1024 * 1024
        ),
        cost_estimate=pl.CostEstimate(
            flops=2 * 10**9, bytes_accessed=8 * 10**6, transcendentals=655360
        ),
    )(
        cache_count,
        block,
        routes.T,
        query,
        own_kv,
        own_cache,
        residual,
        gain[None, :],
        jnp.asarray(spread, jnp.bfloat16),
        jnp.asarray(wanted),
    )


def pack_weights_kernel(gate_up_ref, down_ref, out_ref):
    depth, both = gate_up_ref.shape
    pieces = both // HDIM
    tall = down_ref.shape[0] // pieces
    out_ref[:depth, :] = gate_up_ref[...]
    for one in range(pieces):
        out_ref[depth:, one * HDIM : (one + 1) * HDIM] = down_ref[one * tall : (one + 1) * tall, :]


def pack_weights(gate_up, down_proj):
    depth, both = gate_up.shape
    tall = down_proj.shape[0] * HDIM // both
    vmem = pl.BlockSpec(memory_space=pltpu.VMEM)
    return pl.pallas_call(
        pack_weights_kernel,
        out_shape=jax.ShapeDtypeStruct((depth + tall, both), gate_up.dtype),
        in_specs=[vmem, vmem],
        out_specs=vmem,
        compiler_params=pltpu.CompilerParams(vmem_limit_bytes=63 * 1024 * 1024),
    )(gate_up, down_proj)


def expert_kernel(
    arrived_ref,
    weight_hbm,
    out_ref,
    weight_ref,
    rows_ref,
    total_ref,
    sent_ref,
    load_sem,
    send_sem,
    recv_sem,
):
    layers, across, block, width = arrived_ref.shape
    shards, _, both = weight_ref.shape
    hidden = both // 2
    depth = HALVES * width // shards
    fold = hidden * HDIM // both
    tile = 2 * HDIM
    main = block // HALVES // SUB * SUB
    rest = block // HALVES - main
    pair = 2
    tall = layers * main
    low = layers * HALVES * rest
    me = lax.axis_index("exp")
    my_layer = me // across
    my_place = me % across
    loads = []
    for part in range(4):
        span = slice(part * shards // 4, (part + 1) * shards // 4)
        load = pltpu.make_async_copy(weight_hbm.at[span], weight_ref.at[span], load_sem.at[part])
        load.start()
        loads.append(load)
    barrier = pltpu.get_barrier_semaphore()
    for offset in range(1, layers * across):
        pl.semaphore_signal(
            barrier,
            inc=1,
            device_id={"exp": (me + offset) % (layers * across)},
            device_id_type=pl.DeviceIdType.MESH,
        )
    copies = []
    for chunk in range(across // pair):
        for one in range(pair):
            place = (my_place + chunk * pair + one) % across
            top = slice(one * tall, (one + 1) * tall)
            end = slice(pair * tall + one * low, pair * tall + (one + 1) * low)
            rows_ref[top, :width] = arrived_ref[:, place, :main, :].reshape(tall, width)
            rows_ref[top, width:] = arrived_ref[:, place, main : HALVES * main, :].reshape(
                tall, width
            )
            tail = arrived_ref[:, place, HALVES * main :, :].astype(jnp.float32)
            swapped = jnp.concatenate([tail[:, rest:], tail[:, :rest]], axis=1)
            rows_ref[end, :width] = tail.reshape(low, width).astype(jnp.bfloat16)
            rows_ref[end, width:] = swapped.reshape(low, width).astype(jnp.bfloat16)
        if chunk == 0:
            for load in loads:
                load.wait()
        rows = rows_ref[...]
        for step in range(hidden // tile):
            at = step * tile
            gate_weight = weight_ref[:, :depth, at : at + tile]
            up_weight = weight_ref[:, :depth, hidden + at : hidden + at + tile]
            gate = jnp.dot(
                rows, gate_weight.reshape(shards * depth, tile), preferred_element_type=jnp.float32
            )
            up = jnp.dot(
                rows, up_weight.reshape(shards * depth, tile), preferred_element_type=jnp.float32
            )
            activated = (gate / (1.0 + jnp.exp(-gate)) * up).astype(jnp.bfloat16)
            first = at // fold
            down = jnp.concatenate(
                [
                    jnp.concatenate(
                        [
                            weight_ref[shard, depth:, piece * HDIM : (piece + 1) * HDIM]
                            for piece in range(first, first + tile // fold)
                        ],
                        axis=0,
                    )
                    for shard in range(shards)
                ],
                axis=1,
            )
            result = jnp.dot(activated, down, preferred_element_type=jnp.float32)
            if step == 0:
                total_ref[...] = result
            else:
                total_ref[...] = total_ref[...] + result
        for one in range(pair):
            turn = chunk * pair + one
            top = slice(one * tall, (one + 1) * tall)
            end = slice(pair * tall + one * low, pair * tall + (one + 1) * low)
            sent_ref[turn, :, :main, :] = (
                total_ref[top, :width].astype(jnp.bfloat16).reshape(layers, main, width)
            )
            sent_ref[turn, :, main : HALVES * main, :] = (
                total_ref[top, width:].astype(jnp.bfloat16).reshape(layers, main, width)
            )
            left = total_ref[end, :width].reshape(layers, HALVES * rest, width)
            right = total_ref[end, width:].reshape(layers, HALVES * rest, width)
            sent_ref[turn, :, HALVES * main :, :] = jnp.concatenate(
                [left[:, :rest], right[:, :rest]], axis=1
            ).astype(jnp.bfloat16)
        if chunk == 0:
            pl.semaphore_wait(barrier, layers * across - 1)
        far_first = sorted(range(layers), key=lambda hop: -min(hop, layers - hop))
        for hop in far_first:
            for one in range(pair):
                turn = chunk * pair + one
                place = (my_place + turn) % across
                layer = (my_layer + hop) % layers
                if turn == 0 and hop == 0:
                    copy = pltpu.make_async_copy(
                        sent_ref.at[turn, layer], out_ref.at[me], load_sem.at[4]
                    )
                else:
                    copy = pltpu.make_async_remote_copy(
                        src_ref=sent_ref.at[turn, layer],
                        dst_ref=out_ref.at[me],
                        send_sem=send_sem.at[turn, hop],
                        recv_sem=recv_sem.at[turn, hop],
                        device_id={"exp": layer * across + place},
                        device_id_type=pl.DeviceIdType.MESH,
                    )
                copy.start()
                copies.append(copy)
    for copy in copies:
        copy.wait()


def expert_and_return(arrived, weights, across):
    sources, block, width = arrived.shape
    layers = sources // across
    both = weights.shape[2]
    row_total = sources // across * 2 * (block // HALVES + block // HALVES % SUB)
    outside = pl.BlockSpec(memory_space=pltpu.HBM)
    return pl.pallas_call(
        expert_kernel,
        out_shape=jax.ShapeDtypeStruct(arrived.shape, jnp.bfloat16),
        in_specs=[pl.BlockSpec(memory_space=pltpu.VMEM), outside],
        out_specs=outside,
        scratch_shapes=[
            pltpu.VMEM(weights.shape, jnp.bfloat16),
            pltpu.VMEM((row_total, HALVES * width), jnp.bfloat16),
            pltpu.VMEM((row_total, HALVES * width), jnp.float32),
            pltpu.VMEM((across, layers, block, width), jnp.bfloat16),
            pltpu.SemaphoreType.DMA((5,)),
            pltpu.SemaphoreType.DMA((across, layers)),
            pltpu.SemaphoreType.DMA((across, layers)),
        ],
        compiler_params=pltpu.CompilerParams(
            collective_id=1, has_side_effects=True, vmem_limit_bytes=56 * 1024 * 1024
        ),
        cost_estimate=pl.CostEstimate(
            flops=7 * 10**9, bytes_accessed=15 * 10**6, transcendentals=589824
        ),
    )(arrived.reshape(layers, across, block, width), weights)


def body(
    new_q,
    new_kv,
    cache_kv,
    cache_len,
    prompt_kv,
    prompt_len,
    residual,
    norm_gain,
    routes,
    route_weight,
    gate_up,
    down_proj,
):
    experts_here = lax.axis_size("exp")
    token_count = new_q.shape[0]
    capacity = token_count * TOP * 5 // (4 * experts_here)
    spread, half, slot = slot_layout(experts_here, capacity)
    chosen = membership(routes, experts_here)
    codes = slot_codes(chosen, spread)
    weights = lax.all_gather(pack_weights(gate_up[0], down_proj[0]), "req", axis=0)
    stream, outbox = attend_and_pack(
        new_q,
        new_kv,
        cache_kv,
        cache_len,
        prompt_kv,
        prompt_len,
        residual,
        norm_gain,
        routes,
        experts_here,
        capacity,
    )
    outbox = outbox.reshape(experts_here, HALVES * capacity, -1)
    arrived = lax.all_to_all(outbox, "exp", split_axis=0, concat_axis=0, tiled=True)
    returned = expert_and_return(arrived, weights, ACROSS)
    returned = returned.reshape(-1, returned.shape[-1])
    combined = combine_rows(returned, chosen, route_weight, codes, spread, half, slot)
    return (stream + combined).astype(jnp.bfloat16)


def solution(mesh):
    return jax.shard_map(
        body,
        mesh=mesh,
        in_specs=(
            P(("req", "exp"), None),
            P(("req", "exp"), None),
            P(("req", "exp"), None),
            P(("req", "exp")),
            P(("req", "exp"), None),
            P(("req", "exp")),
            P(("req", "exp"), None),
            P(),
            P(("req", "exp"), None),
            P(("req", "exp"), None),
            P("exp", "req", None),
            P("exp", None, "req"),
        ),
        out_specs=P(("req", "exp"), None),
        check_vma=False,
    )
```
